32 devices in a mesh: strip: 4 (over z), cross: 8 (over y, x, core).
Axes of the slice: x: 2, y: 2, z: 4, core: 2. Of those that a mesh axis runs over, the one named last changes fastest.
Arguments:
- rhs: bfloat16 [4, 64, 14336], P('strip', None, 'cross'), may hold values from -6 to 6
- inverse: bfloat16 [4, 8, 1792, 1792], P('strip', 'cross'), may hold values from -2 to 2
- dis_fwd: bfloat16 [4, 8, 256, 1792], P('strip', 'cross'), may hold values from -0.1875 to 0.1875
- agg_fwd: bfloat16 [4, 14336, 256], P('strip', 'cross'), may hold values from -0.0625 to 0.0625
- phase_fwd: float32 [4, 128], P('strip'), may hold values from -3.140625 to 3.140625
- gain_fwd: float32 [4, 128], P('strip'), may hold values from 0.5 to 1
- dis_back: bfloat16 [4, 8, 256, 1792], P('strip', 'cross'), may hold values from -0.1875 to 0.1875
- agg_back: bfloat16 [4, 14336, 256], P('strip', 'cross'), may hold values from -0.0625 to 0.0625
- phase_back: float32 [4, 128], P('strip'), may hold values from -3.140625 to 3.140625
- gain_back: float32 [4, 128], P('strip'), may hold values from 0.5 to 1
Outputs:
- first_pass: float32 [4, 64, 14336], P('strip', None, 'cross')
- solution: float32 [4, 64, 14336], P('strip', None, 'cross')
The draws below stay inside these ranges and needn't reach their ends.
All inputs are finite; a program needn't handle non-finite values.
Results may differ from the reference program's by a relative error of at most 0.04.
Values may be sent and summed in bfloat16 or wider, within the bound.
A program may use at most 64 MiB of HBM per device.

```python
import math
import jax
import jax.numpy as jnp
from jax import lax

UNK = 1792
MODES = 256
HALF = 128
ANGLES = 64
STRIPS = 4
CLUSTERS = 8
ROW = 14336


def draw_inverse(key, part):
    diag_key = jax.random.fold_in(key, 11)
    off_key = jax.random.fold_in(key, 12)
    diag_scale = jax.random.uniform(diag_key, (STRIPS, CLUSTERS, UNK), jnp.float32, 0.5, 1.5)
    spread = jnp.clip(jax.random.normal(off_key, (STRIPS, CLUSTERS, UNK, UNK), jnp.float32), -4.0, 4.0) * (0.5 / UNK ** 0.5)
    identity = jnp.eye(UNK, dtype=jnp.float32)
    return (spread + identity * diag_scale[..., None]).astype(jnp.bfloat16)


def with_spikes(drawn, stream_key, source, target, blocks, factor):
    owner, partner = [(jnp.arange(drawn.shape[dim]) // (drawn.shape[dim] // blocks)).reshape([-1 if axis == dim else 1 for axis in range(drawn.ndim)]) for dim in (source, target)]
    chosen = jax.random.permutation(stream_key, blocks)[partner]
    strong = (owner == chosen) | (owner == (partner + blocks // 2) % blocks)
    return jnp.where(strong, factor * drawn, drawn)


def levels(own_key, shape, shards, low, largest):
    def one(axis_at, parts):
        draws = jax.random.uniform(jax.random.fold_in(jax.random.fold_in(own_key, 6), axis_at), (parts,), jnp.float32, low / len(shards), largest / len(shards))
        return jnp.repeat(jnp.exp(draws), shape[axis_at] // parts).reshape((-1,) + (1,) * (len(shape) - axis_at - 1))

    level = one(*shards[0])
    for cut in shards[1:]:
        level = level * one(*cut)
    return level


def noise(stream_key, dims, scale, reach, pieces=(), kind=jnp.bfloat16):
    result = jax.random.normal(stream_key, dims, jnp.float32) * scale
    if len(pieces) > 0:
        result = levels(stream_key, dims, pieces, -0.22, 0.18) * result
    return jnp.clip(result, min=-reach, max=reach).astype(kind)


def heavy_noise(own_key, dims, width, most, cuts, heavy, kind=jnp.bfloat16):
    values = width * jax.random.normal(own_key, dims, jnp.float32)
    if cuts:
        values = values * levels(own_key, dims, cuts, -0.22, 0.18)
    return jnp.clip(with_spikes(values, jax.random.fold_in(own_key, 3), *heavy), -most, most).astype(kind)


def setup_inputs(seed: int = 0) -> dict:
    key_list = jax.random.split(jax.random.key(seed), 11)
    return {
        "rhs": noise(key_list[0], (STRIPS, ANGLES, ROW), 1.0, 6.0, ((0, 4), (2, 8))),
        "inverse": draw_inverse(jax.random.fold_in(key_list[10], 71), 0),
        "dis_fwd": noise(key_list[2], (STRIPS, CLUSTERS, MODES, UNK), (0.5 * MODES ** -0.5), 0.1875, ((0, 4), (1, 8))),
        "agg_fwd": heavy_noise(key_list[3], (STRIPS, ROW, MODES), ROW ** -0.5, 0.0625, ((0, 4), (1, 8)), (1, 2, 8, 2.0)),
        "phase_fwd": jnp.clip(jax.random.uniform(key_list[4], (STRIPS, HALF), jnp.float32, -3.140625, 3.140625), -3.140625, 3.140625),
        "gain_fwd": jnp.clip(jnp.exp(math.log(1.0) - 0.6931472 * jax.random.uniform(key_list[5], (STRIPS, HALF), jnp.float32) ** levels(key_list[5], (STRIPS, HALF), ((0, 4),), -0.2, 0.2)), 0.5, 1.0),
        "dis_back": noise(key_list[6], (STRIPS, CLUSTERS, MODES, UNK), (0.5 * MODES ** -0.5), 0.1875, ((0, 4), (1, 8))),
        "agg_back": heavy_noise(key_list[7], (STRIPS, ROW, MODES), ROW ** -0.5, 0.0625, ((0, 4), (1, 8)), (1, 2, 8, 2.0)),
        "phase_back": jnp.clip(jax.random.uniform(key_list[8], (STRIPS, HALF), jnp.float32, -3.140625, 3.140625), -3.140625, 3.140625),
        "gain_back": jnp.clip(jnp.exp(math.log(1.0) - 0.6931472 * jax.random.uniform(key_list[9], (STRIPS, HALF), jnp.float32) ** levels(key_list[9], (STRIPS, HALF), ((0, 4),), -0.2, 0.2)), 0.5, 1.0),
    }


def rotate(carry, phase, gain):
    half = phase.shape[0]
    real_part = carry[:, :half]
    imag_part = carry[:, half:]
    cosine = jnp.cos(phase)
    sine = jnp.sin(phase)
    return jnp.concatenate([gain * (cosine * real_part - sine * imag_part), gain * (sine * real_part + cosine * imag_part)], axis=1)


def rounded(value):
    return lax.optimization_barrier(value.astype(jnp.bfloat16)).astype(jnp.float32)


def strip_solve(source, carried, inv_strip, dis_strip, agg_strip):
    angles, row = source.shape
    clusters, unk = inv_strip.shape[0], inv_strip.shape[1]
    spread = jnp.einsum("am,cmu->acu", rounded(carried), dis_strip.astype(jnp.float32), precision=lax.Precision.HIGHEST).reshape(angles, row)
    field = source - spread
    answer = jnp.einsum("acv,cvu->acu", rounded(field).reshape(angles, clusters, unk), inv_strip.astype(jnp.float32), precision=lax.Precision.HIGHEST).reshape(angles, row)
    summed = jnp.dot(answer.astype(jnp.bfloat16), agg_strip, preferred_element_type=jnp.float32)
    return field, answer, summed


def reference(rhs, inverse, dis_fwd, agg_fwd, phase_fwd, gain_fwd, dis_back, agg_back, phase_back, gain_back):
    strips, angles, row = rhs.shape
    modes = dis_fwd.shape[2]
    carry = jnp.zeros((angles, modes), jnp.float32)
    fields = []
    firsts = []
    for strip in range(strips):
        field, answer, summed = strip_solve(rhs[strip].astype(jnp.float32), carry, inverse[strip], dis_fwd[strip], agg_fwd[strip])
        fields.append(field)
        firsts.append(answer)
        carry = rotate(carry, phase_fwd[strip], gain_fwd[strip]) + summed
    carry = jnp.zeros((angles, modes), jnp.float32)
    seconds = [None] * strips
    for strip in range(strips - 1, -1, -1):
        field, answer, summed = strip_solve(fields[strip], carry, inverse[strip], dis_back[strip], agg_back[strip])
        seconds[strip] = answer
        carry = rotate(carry, phase_back[strip], gain_back[strip]) + summed
    return jnp.stack(firsts), jnp.stack(seconds)
```

```python
import functools

import jax
import jax.numpy as jnp
from jax import lax
from jax.experimental import pallas as pl
from jax.experimental.pallas import tpu as pltpu
from jax.sharding import PartitionSpec as P

MESH = pl.DeviceIdType.MESH
BF = jnp.bfloat16
F32 = jnp.float32
KINDS = 16
(
    T_RS, T_AG, M_RS, M_AG, N_RS, N_AG, L_RS, L_AG,
    B_RS, Q_RS, R_RS, C_IN, C_ON, C_SH, D_ON, D_SH,
) = range(KINDS)


def dot(a, b):
    return jnp.dot(a, b, preferred_element_type=F32)


def kernel(
    strips, n, width,
    rhs, inverse, dis_fwd, agg_fwd, phase_fwd, gain_fwd, dis_back, agg_back, phase_back, gain_back,
    first_ref, second_ref,
    x_f, x_b, inv, agg_f, agg_b, p, z, u_b,
    t_own, t_out, t_in, m_own, m_out, m_in, n_own, n_out, n_in, l_in, t_all, m_all, n_all, l_all,
    b_own, b_out, b_in, q_own, q_out, q_in, r_in, c_in,
    c_out, c_all, d_out, d_all,
    turns, coef, load_sem, sems,
):
    s = lax.axis_index("strip")
    me = lax.axis_index("cross")
    is_first = s == 0
    is_direct = s == 1
    is_last = s == strips - 1
    is_turn = s == strips - 2
    inner = jnp.logical_and(s > 1, s < strips - 1)
    angles = rhs.shape[1]
    modes = agg_f.shape[1]
    half = modes // 2
    unk = p.shape[1]
    blocks = unk // width

    barrier = pltpu.get_barrier_semaphore()

    def greet(strip, peer):
        pl.semaphore_signal(barrier, inc=1, device_id=(strip, peer), device_id_type=MESH)

    def others(fn):
        def step(j, carry):
            fn(lax.rem(me + j, n))
            return carry
        lax.fori_loop(1, n, step, 0)

    def everyone(fn):
        def step(j, carry):
            fn(lax.rem(me + j, n))
            return carry
        lax.fori_loop(0, n, step, 0)

    load_rhs = pltpu.make_async_copy(rhs.at[0], x_f.at[pl.ds(0, angles)], load_sem.at[0])
    load_dis = pltpu.make_async_copy(
        dis_fwd.at[0, 0], x_f.at[pl.ds(angles, modes)], load_sem.at[1]
    )
    load_agg = pltpu.make_async_copy(agg_fwd.at[0], agg_f, load_sem.at[2])
    load_dis_b = pltpu.make_async_copy(dis_back.at[0, 0], x_b, load_sem.at[3])
    load_agg_b = pltpu.make_async_copy(agg_back.at[0], agg_b, load_sem.at[4])
    inv_loads = [
        pltpu.make_async_copy(
            inverse.at[0, 0, :, pl.ds(j * width, width)], inv.at[j], load_sem.at[5 + j]
        )
        for j in range(blocks)
    ]
    turn_loads = [
        pltpu.make_async_copy(ref, turns.at[j], load_sem.at[5 + blocks + j])
        for j, ref in enumerate((phase_fwd, gain_fwd, phase_back, gain_back))
    ]
    load_rhs.start()

    @pl.when(s > 0)
    def _():
        load_dis.start()

    for copy in inv_loads:
        copy.start()

    @pl.when(s > 0)
    def _():
        everyone(lambda peer: greet(s - 1, peer))

    @pl.when(s < strips - 1)
    def _():
        everyone(lambda peer: greet(s + 1, peer))

    others(lambda peer: greet(s, peer))

    @pl.when(s < strips - 1)
    def _():
        load_agg.start()

    @pl.when(s > 0)
    def _():
        load_agg_b.start()

    @pl.when(s < strips - 1)
    def _():
        load_dis_b.start()

    for copy in turn_loads:
        copy.start()

    def remote(kind, src, dst, strip, peer):
        return pltpu.make_async_remote_copy(
            src_ref=src,
            dst_ref=dst,
            send_sem=sems.at[kind, 0, peer],
            recv_sem=sems.at[kind, 1, me],
            device_id=(strip, peer),
            device_id_type=MESH,
        )

    def arrived(kind, dst, peer):
        pltpu.make_async_remote_copy(
            src_ref=dst.at[peer],
            dst_ref=dst.at[peer],
            send_sem=sems.at[kind, 0, peer],
            recv_sem=sems.at[kind, 1, peer],
            device_id=(s, peer),
            device_id_type=MESH,
        ).wait_recv()

    def scatter(kind, out, into):
        others(lambda peer: remote(kind, out.at[peer], into.at[me], s, peer).start())

    def scatter_sent(kind, out, into):
        others(lambda peer: remote(kind, out.at[peer], into.at[me], s, peer).wait_send())

    def cross_scatter(kind, out, into, strip):
        everyone(lambda peer: remote(kind, out.at[peer], into.at[me], strip, peer).start())

    def cross_scatter_sent(kind, out, into, strip):
        everyone(lambda peer: remote(kind, out.at[peer], into.at[me], strip, peer).wait_send())

    def spread(kind, src, into, strip):
        everyone(lambda peer: remote(kind, src, into.at[me], strip, peer).start())

    def spread_sent(kind, src, into, strip):
        everyone(lambda peer: remote(kind, src, into.at[me], strip, peer).wait_send())

    def total(kind, own, into):
        others(lambda peer: arrived(kind, into, peer))
        value = own[me]
        for j in range(1, n):
            value = value + into[lax.rem(me + j, n)].astype(F32)
        return value

    def cross_total(kind, into):
        everyone(lambda peer: arrived(kind, into, peer))
        value = into[0].astype(F32)
        for j in range(1, n):
            value = value + into[j].astype(F32)
        return value

    def share(kind, buf):
        others(lambda peer: remote(kind, buf.at[me], buf.at[me], s, peer).start())

    def share_sent(kind, buf):
        others(lambda peer: remote(kind, buf.at[me], buf.at[me], s, peer).wait_send())

    def shared(kind, buf):
        others(lambda peer: arrived(kind, buf, peer))

    def split(value, own, out):
        part = value.shape[0] // n
        for k in range(n):
            piece = value[k * part:(k + 1) * part]
            own[k] = piece
            out[k] = piece.astype(BF)

    def joined(buf):
        return jnp.concatenate([buf[k] for k in range(n)], axis=0)

    def rotated(value, at):
        real, imag = value[:, :half], value[:, half:]
        cosine, sine = coef[at], coef[at + 1]
        return jnp.concatenate(
            [cosine * real - sine * imag, sine * real + cosine * imag], axis=1
        )

    def columns(j):
        return slice(j * width, (j + 1) * width)

    def back_matrix():
        for j in range(blocks):
            u_b[:, columns(j)] = dot(x_b[...], inv[j]).astype(BF)

    load_rhs.wait()

    @pl.when(is_first)
    def _():
        for j in range(blocks):
            inv_loads[j].wait()
            product = dot(x_f[:angles], inv[j])
            p[:, columns(j)] = product
            z[:angles, columns(j)] = product.astype(BF)
        load_agg.wait()
        split(dot(z[:angles], agg_f[...]), b_own, b_out)

    @pl.when(s > 0)
    def _():
        load_dis.wait()
        for j in range(blocks):
            inv_loads[j].wait()
            product = dot(x_f[...], inv[j])
            p[:, columns(j)] = product[:angles]
            z[:, columns(j)] = product.astype(BF)

    greeted = (n - 1) + jnp.where(s > 0, n, 0) + jnp.where(s < strips - 1, n, 0)
    pl.semaphore_wait(barrier, greeted)

    @pl.when(is_first)
    def _():
        cross_scatter(C_IN, b_out, c_in, s + 1)
        load_dis_b.wait()
        back_matrix()
        first_ref[0] = p[...]

    @pl.when(inner)
    def _():
        load_agg.wait()
        value = dot(z[...], agg_f[...])
        split(value[angles:], t_own, t_out)
        split(value[:angles], b_own, b_out)
        scatter(T_RS, t_out, t_in)

    @pl.when(s > 1)
    def _():
        load_agg_b.wait()
        value = dot(z[...], agg_b[...])
        split(value[angles:], m_own, m_out)
        split(value[:angles], q_own, q_out)

    @pl.when(is_last)
    def _():
        cross_scatter(L_RS, m_out, l_in, s - 1)
        cross_scatter(R_RS, q_out, r_in, s - 1)

    @pl.when(inner)
    def _():
        scatter(B_RS, b_out, b_in)
        scatter(M_RS, m_out, m_in)
        scatter(Q_RS, q_out, q_in)

    for copy in turn_loads:
        copy.wait()
    for at in (0, 2):
        coef[at] = jnp.cos(turns[at]) * turns[at + 1]
        coef[at + 1] = jnp.sin(turns[at]) * turns[at + 1]

    @pl.when(inner)
    def _():
        load_dis_b.wait()
        back_matrix()
        split(dot(u_b[...], agg_b[...]), n_own, n_out)
        scatter(N_RS, n_out, n_in)
        t_all[me] = total(T_RS, t_own, t_in).astype(BF)
        share(T_AG, t_all)
        m_all[me] = total(M_RS, m_own, m_in).astype(BF)
        share(M_AG, m_all)

    @pl.when(is_turn)
    def _():
        l_all[me] = cross_total(L_RS, l_in).astype(BF)
        share(L_AG, l_all)

    @pl.when(inner)
    def _():
        n_all[me] = total(N_RS, n_own, n_in).astype(BF)
        share(N_AG, n_all)
        b_own[me] = total(B_RS, b_own, b_in)
        q_own[me] = total(Q_RS, q_own, q_in)

    @pl.when(is_direct)
    def _():
        load_dis_b.wait()
        back_matrix()
        c_all[me] = cross_total(C_IN, c_in).astype(BF)
        share(C_SH, c_all)
        load_agg_b.wait()
        split(dot(u_b[...], agg_b[...]), n_own, n_out)
        scatter(N_RS, n_out, n_in)
        load_agg.wait()
        shared(C_SH, c_all)
        first_ref[0] = p[...] - dot(joined(c_all), z[angles:])
        rounded = first_ref[0].astype(BF)
        split(dot(rounded, agg_f[...]), b_own, b_out)
        leaving = b_own[me] + rotated(c_all[me].astype(F32), 0)
        b_out[me] = leaving.astype(BF)
        cross_scatter(C_IN, b_out, c_in, s + 1)
        split(dot(rounded, agg_b[...]), q_own, q_out)
        scatter(Q_RS, q_out, q_in)
        n_all[me] = total(N_RS, n_own, n_in).astype(BF)
        share(N_AG, n_all)
        q_own[me] = total(Q_RS, q_own, q_in)
        shared(N_AG, n_all)

    @pl.when(inner)
    def _():
        shared(T_AG, t_all)
        shared(M_AG, m_all)

        @pl.when(s == 2)
        def _():
            c_all[me] = cross_total(C_IN, c_in).astype(BF)

        @pl.when(s > 2)
        def _():
            arrived(C_ON, c_all, me)

        held = c_all[me]
        leaving = rotated(held.astype(F32), 0) + b_own[me]
        c_out[...] = (leaving - dot(held, joined(t_all))).astype(BF)

        @pl.when(is_turn)
        def _():
            spread(C_ON, c_out, c_all, s + 1)

        @pl.when(s < strips - 2)
        def _():
            remote(C_ON, c_out, c_all.at[me], s + 1, me).start()

        q_own[me] = q_own[me] - dot(held, joined(m_all))

    @pl.when(is_turn)
    def _():
        turned = cross_total(R_RS, r_in)
        shared(L_AG, l_all)
        d_all[me] = (turned - dot(c_out[...], joined(l_all))).astype(BF)

    @pl.when(inner)
    def _():
        shared(N_AG, n_all)

    @pl.when(jnp.logical_and(s > 0, s < strips - 2))
    def _():
        arrived(D_ON, d_all, me)

    @pl.when(jnp.logical_and(s > 0, s < strips - 1))
    def _():
        held = d_all[me]
        leaving = rotated(held.astype(F32), 2) + q_own[me]
        d_out[...] = (leaving - dot(held, joined(n_all))).astype(BF)

        @pl.when(is_direct)
        def _():
            spread(D_ON, d_out, d_all, s - 1)

        @pl.when(s > 1)
        def _():
            remote(D_ON, d_out, d_all.at[me], s - 1, me).start()
            share(C_SH, c_all)

        share(D_SH, d_all)

    @pl.when(is_last)
    def _():
        everyone(lambda peer: arrived(C_ON, c_all, peer))

    @pl.when(inner)
    def _():
        shared(C_SH, c_all)

    @pl.when(s > 1)
    def _():
        first_ref[0] = p[...] - dot(joined(c_all), z[angles:])

    @pl.when(is_last)
    def _():
        second_ref[0] = first_ref[0]

    @pl.when(is_first)
    def _():
        everyone(lambda peer: arrived(D_ON, d_all, peer))

    @pl.when(jnp.logical_and(s > 0, s < strips - 1))
    def _():
        shared(D_SH, d_all)

    @pl.when(s < strips - 1)
    def _():
        second_ref[0] = first_ref[0] - dot(joined(d_all), u_b[...])

    @pl.when(s < 2)
    def _():
        cross_scatter_sent(C_IN, b_out, c_in, s + 1)

    @pl.when(inner)
    def _():
        scatter_sent(T_RS, t_out, t_in)
        share_sent(T_AG, t_all)
        scatter_sent(M_RS, m_out, m_in)
        share_sent(M_AG, m_all)
        scatter_sent(B_RS, b_out, b_in)

    @pl.when(jnp.logical_and(s > 0, s < strips - 1))
    def _():
        scatter_sent(N_RS, n_out, n_in)
        share_sent(N_AG, n_all)
        scatter_sent(Q_RS, q_out, q_in)
        share_sent(C_SH, c_all)
        share_sent(D_SH, d_all)

    @pl.when(is_turn)
    def _():
        share_sent(L_AG, l_all)
        spread_sent(C_ON, c_out, c_all, s + 1)

    @pl.when(jnp.logical_and(s > 1, s < strips - 2))
    def _():
        remote(C_ON, c_out, c_all.at[me], s + 1, me).wait_send()

    @pl.when(is_direct)
    def _():
        spread_sent(D_ON, d_out, d_all, s - 1)

    @pl.when(inner)
    def _():
        remote(D_ON, d_out, d_all.at[me], s - 1, me).wait_send()

    @pl.when(is_last)
    def _():
        cross_scatter_sent(L_RS, m_out, l_in, s - 1)
        cross_scatter_sent(R_RS, q_out, r_in, s - 1)


def body(strips, n, rhs, inverse, dis_fwd, agg_fwd, phase_fwd, gain_fwd, dis_back, agg_back, phase_back, gain_back):
    _, angles, unk = rhs.shape
    modes = agg_fwd.shape[2]
    width = 256 if unk % 256 == 0 else unk
    blocks = unk // width
    rows, part = angles // n, modes // n
    hbm = pl.BlockSpec(memory_space=pl.ANY)
    vmem = pl.BlockSpec(memory_space=pltpu.VMEM)
    out = pltpu.VMEM((1, angles, unk), F32)
    return pl.pallas_call(
        functools.partial(kernel, strips, n, width),
        out_shape=(out, out),
        in_specs=[hbm] * 10,
        out_specs=(vmem, vmem),
        scratch_shapes=[
            pltpu.VMEM((angles + modes, unk), BF),
            pltpu.VMEM((modes, unk), BF),
            pltpu.VMEM((blocks, unk, width), BF),
            pltpu.VMEM((unk, modes), BF),
            pltpu.VMEM((unk, modes), BF),
            pltpu.VMEM((angles, unk), F32),
            pltpu.VMEM((angles + modes, unk), BF),
            pltpu.VMEM((modes, unk), BF),
        ]
        + [pltpu.VMEM((n, part, modes), kind) for kind in (F32, BF, BF) * 3 + (BF,) * 5]
        + [pltpu.VMEM((n, rows, modes), kind) for kind in (F32, BF, BF) * 2 + (BF, BF)]
        + [pltpu.VMEM((rows, modes), BF), pltpu.VMEM((n, rows, modes), BF)] * 2
        + [pltpu.VMEM((4, 1, modes // 2), F32)] * 2
        + [pltpu.SemaphoreType.DMA((9 + blocks,)), pltpu.SemaphoreType.DMA((KINDS, 2, n))],
        compiler_params=pltpu.CompilerParams(
            collective_id=0, has_side_effects=True, vmem_limit_bytes=60 * 1024 * 1024
        ),
    )(rhs, inverse, dis_fwd, agg_fwd, phase_fwd, gain_fwd, dis_back, agg_back, phase_back, gain_back)


def solution(mesh):
    strips, n = mesh.shape["strip"], mesh.shape["cross"]
    return jax.shard_map(
        functools.partial(body, strips, n),
        mesh=mesh,
        in_specs=(
            P("strip", None, "cross"),
            P("strip", "cross", None, None),
            P("strip", "cross", None, None),
            P("strip", "cross", None),
            P("strip", None),
            P("strip", None),
            P("strip", "cross", None, None),
            P("strip", "cross", None),
            P("strip", None),
            P("strip", None),
        ),
        out_specs=(P("strip", None, "cross"), P("strip", None, "cross")),
        check_vma=False,
    )
```

```python
import functools

import jax
import jax.numpy as jnp
from jax import lax
from jax.experimental import pallas as pl
from jax.experimental.pallas import tpu as pltpu
from jax.sharding import PartitionSpec as P

MESH = pl.DeviceIdType.MESH
BF = jnp.bfloat16
F32 = jnp.float32
KINDS = 16
(
    T_RS, T_AG, M_RS, M_AG, N_RS, N_AG, L_RS, L_AG,
    B_RS, Q_RS, R_RS, C_IN, C_ON, C_SH, D_ON, D_SH,
) = range(KINDS)


def dot(a, b):
    return jnp.dot(a, b, preferred_element_type=F32)


def kernel(
    strips, n, width,
    rhs, inverse, dis_fwd, agg_fwd, phase_fwd, gain_fwd, dis_back, agg_back, phase_back, gain_back,
    first_ref, second_ref,
    x_r, x_f, x_b, inv, agg_f, agg_b, p, z, u_f, u_b,
    t_own, t_out, t_in, m_own, m_out, m_in, n_own, n_out, n_in, l_in, t_all, m_all, n_all, l_all,
    b_own, b_out, b_in, q_own, q_out, q_in, r_in, c_in,
    c_out, c_all, d_out, d_all,
    turns, coef, load_sem, sems,
):
    s = lax.axis_index("strip")
    me = lax.axis_index("cross")
    is_first = s == 0
    is_direct = s == 1
    is_last = s == strips - 1
    is_turn = s == strips - 2
    inner = jnp.logical_and(s > 1, s < strips - 1)
    angles = rhs.shape[1]
    modes = agg_f.shape[1]
    half = modes // 2
    unk = p.shape[1]
    blocks = unk // width
    leaders = n // 2
    slot = me // 2
    follows = lax.rem(me, 2)
    leads = follows == 0

    barrier = pltpu.get_barrier_semaphore()

    def greet(strip, peer):
        pl.semaphore_signal(barrier, inc=1, device_id=(strip, peer), device_id_type=MESH)

    def others(fn):
        def step(j, carry):
            fn(lax.rem(me + j, n))
            return carry
        lax.fori_loop(1, n, step, 0)

    def everyone(fn):
        def step(j, carry):
            fn(lax.rem(me + j, n))
            return carry
        lax.fori_loop(0, n, step, 0)

    load_rhs = pltpu.make_async_copy(rhs.at[0], x_r, load_sem.at[0])
    load_dis = pltpu.make_async_copy(dis_fwd.at[0, 0], x_f, load_sem.at[1])
    load_agg = pltpu.make_async_copy(agg_fwd.at[0], agg_f, load_sem.at[2])
    load_dis_b = pltpu.make_async_copy(dis_back.at[0, 0], x_b, load_sem.at[3])
    load_agg_b = pltpu.make_async_copy(agg_back.at[0], agg_b, load_sem.at[4])
    inv_loads = [
        pltpu.make_async_copy(
            inverse.at[0, 0, :, pl.ds(j * width, width)], inv.at[j], load_sem.at[5 + j]
        )
        for j in range(blocks)
    ]
    turn_loads = [
        pltpu.make_async_copy(ref, turns.at[j], load_sem.at[5 + blocks + j])
        for j, ref in enumerate((phase_fwd, gain_fwd, phase_back, gain_back))
    ]
    @pl.when(is_first)
    def _():
        load_rhs.start()

    @pl.when(s > 0)
    def _():
        load_dis.start()

    for copy in inv_loads:
        copy.start()

    @pl.when(s > 0)
    def _():
        everyone(lambda peer: greet(s - 1, peer))

    @pl.when(s < strips - 1)
    def _():
        everyone(lambda peer: greet(s + 1, peer))

    others(lambda peer: greet(s, peer))

    @pl.when(s < strips - 1)
    def _():
        load_agg.start()

    @pl.when(s > 0)
    def _():
        load_agg_b.start()
        load_rhs.start()

    @pl.when(s < strips - 1)
    def _():
        load_dis_b.start()

    for copy in turn_loads:
        copy.start()

    def remote(kind, src, dst, strip, peer):
        return pltpu.make_async_remote_copy(
            src_ref=src,
            dst_ref=dst,
            send_sem=sems.at[kind, 0, peer],
            recv_sem=sems.at[kind, 1, me],
            device_id=(strip, peer),
            device_id_type=MESH,
        )

    def other_leaders(fn):
        def step(j, carry):
            fn(2 * lax.rem(slot + j, leaders))
            return carry
        lax.fori_loop(1 - follows, leaders, step, 0)

    def every_leader(fn):
        def step(j, carry):
            fn(2 * lax.rem(slot + j, leaders))
            return carry
        lax.fori_loop(0, leaders, step, 0)

    def arrived(kind, dst, peer):
        pltpu.make_async_remote_copy(
            src_ref=dst,
            dst_ref=dst,
            send_sem=sems.at[kind, 0, peer],
            recv_sem=sems.at[kind, 1, peer],
            device_id=(s, peer),
            device_id_type=MESH,
        ).wait_recv()

    def send(copy):
        copy.start()

    def sent(copy):
        copy.wait_send()

    def scatter(kind, out, into, act=send):
        others(lambda peer: act(remote(kind, out.at[peer], into.at[me], s, peer)))

    def cross_scatter(kind, out, into, strip, act=send):
        everyone(lambda peer: act(remote(kind, out.at[peer], into.at[me], strip, peer)))

    def row_scatter(kind, out, into, act=send):
        other_leaders(
            lambda peer: act(remote(kind, out.at[peer // 2], into.at[me], s, peer))
        )

    def cross_row_scatter(kind, out, into, strip, act=send):
        every_leader(
            lambda peer: act(remote(kind, out.at[peer // 2], into.at[me], strip, peer))
        )

    def gather(kind, buf, act=send):
        other_leaders(lambda peer: act(remote(kind, buf.at[me], buf.at[me], s, peer)))

    def share(kind, buf, act=send):
        others(lambda peer: act(remote(kind, buf.at[slot], buf.at[slot], s, peer)))

    def spread(kind, src, into, strip, act=send):
        everyone(lambda peer: act(remote(kind, src, into.at[slot], strip, peer)))

    def hop(kind, src, into, strip, act=send):
        act(remote(kind, src, into.at[slot], strip, me))

    def total(kind, own, into):
        others(lambda peer: arrived(kind, into.at[peer], peer))
        value = own
        for j in range(1, n):
            value = value + into[lax.rem(me + j, n)].astype(F32)
        return value

    def cross_total(kind, into):
        everyone(lambda peer: arrived(kind, into.at[peer], peer))
        value = into[0].astype(F32)
        for j in range(1, n):
            value = value + into[j].astype(F32)
        return value

    def gathered(kind, buf):
        others(lambda peer: arrived(kind, buf.at[peer], peer))

    def shared(kind, buf):
        other_leaders(lambda peer: arrived(kind, buf.at[peer // 2], peer))

    def all_shared(kind, buf):
        every_leader(lambda peer: arrived(kind, buf.at[peer // 2], peer))

    def split(value, own, out):
        pieces = own.shape[0]
        part = value.shape[0] // pieces
        for k in range(pieces):
            piece = value[k * part:(k + 1) * part]
            own[k] = piece
            out[k] = piece.astype(BF)

    def joined(buf):
        return jnp.concatenate([buf[k] for k in range(buf.shape[0])], axis=0)

    def rotated(value, at):
        real, imag = value[:, :half], value[:, half:]
        cosine, sine = coef[at], coef[at + 1]
        return jnp.concatenate(
            [cosine * real - sine * imag, sine * real + cosine * imag], axis=1
        )

    def columns(j):
        return slice(j * width, (j + 1) * width)

    def base_field():
        for j in range(blocks):
            product = dot(x_r[...], inv[j])
            p[:, columns(j)] = product
            z[:, columns(j)] = product.astype(BF)

    def back_matrix():
        for j in range(blocks):
            u_b[:, columns(j)] = dot(x_b[...], inv[j]).astype(BF)

    @pl.when(is_first)
    def _():
        load_rhs.wait()
        inv_loads[0].wait()
        product = dot(x_r[...], inv[0])
        for j in range(blocks):
            if j + 1 < blocks:
                inv_loads[j + 1].wait()
                following = dot(x_r[...], inv[j + 1])
            p[:, columns(j)] = product
            z[:, columns(j)] = product.astype(BF)
            product = following
        load_agg.wait()
        split(dot(z[...], agg_f[...]), b_own, b_out)

    @pl.when(s > 0)
    def _():
        load_dis.wait()
        inv_loads[0].wait()
        product = dot(x_f[...], inv[0])
        for j in range(blocks):
            if j + 1 < blocks:
                inv_loads[j + 1].wait()
                following = dot(x_f[...], inv[j + 1])
            u_f[:, columns(j)] = product.astype(BF)
            product = following

    @pl.when(inner)
    def _():
        load_agg.wait()
        split(dot(u_f[...], agg_f[...]), t_own, t_out)

    @pl.when(s > 0)
    def _():
        load_agg_b.wait()

    @pl.when(is_last)
    def _():
        split(dot(u_f[...], agg_b[...]), m_own, m_out)

    greeted = (n - 1) + jnp.where(s > 0, n, 0) + jnp.where(s < strips - 1, n, 0)
    pl.semaphore_wait(barrier, greeted)

    for copy in turn_loads:
        copy.wait()

    def rotations():
        for at in (0, 2):
            coef[at] = jnp.cos(turns[at]) * turns[at + 1]
            coef[at + 1] = jnp.sin(turns[at]) * turns[at + 1]

    @pl.when(is_first)
    def _():
        cross_row_scatter(C_IN, b_out, c_in, s + 1)
        load_dis_b.wait()
        back_matrix()
        first_ref[0] = p[...]

    @pl.when(inner)
    def _():
        scatter(T_RS, t_out, t_in)
        split(dot(u_f[...], agg_b[...]), m_own, m_out)
        scatter(M_RS, m_out, m_in)
        load_dis_b.wait()
        back_matrix()
        split(dot(u_b[...], agg_b[...]), n_own, n_out)
        scatter(N_RS, n_out, n_in)
        load_rhs.wait()
        rotations()
        t_all[me] = total(T_RS, t_own[me], t_in).astype(BF)
        gather(T_AG, t_all)
        base_field()
        split(dot(z[...], agg_f[...]), b_own, b_out)
        row_scatter(B_RS, b_out, b_in)
        split(dot(z[...], agg_b[...]), q_own, q_out)
        row_scatter(Q_RS, q_out, q_in)

    @pl.when(is_turn)
    def _():
        l_all[me] = cross_total(L_RS, l_in).astype(BF)
        gather(L_AG, l_all)

    @pl.when(inner)
    def _():
        m_all[me] = total(M_RS, m_own[me], m_in).astype(BF)
        gather(M_AG, m_all)
        n_all[me] = total(N_RS, n_own[me], n_in).astype(BF)
        gather(N_AG, n_all)

    @pl.when(is_last)
    def _():
        cross_scatter(L_RS, m_out, l_in, s - 1)
        load_rhs.wait()
        base_field()
        split(dot(z[...], agg_b[...]), q_own, q_out)
        cross_row_scatter(R_RS, q_out, r_in, s - 1)

    @pl.when(is_direct)
    def _():
        load_rhs.wait()
        base_field()
        rotations()

        @pl.when(leads)
        def _():
            c_all[slot] = cross_total(C_IN, c_in).astype(BF)
            share(C_SH, c_all)

        load_dis_b.wait()
        back_matrix()
        load_agg.wait()
        shared(C_SH, c_all)
        first_ref[0] = p[...] - dot(joined(c_all), u_f[...])
        rounded = first_ref[0].astype(BF)
        split(dot(rounded, agg_f[...]), b_own, b_out)

        @pl.when(leads)
        def _():
            leaving = b_own[slot] + rotated(c_all[slot].astype(F32), 0)
            b_out[slot] = leaving.astype(BF)

        cross_row_scatter(C_IN, b_out, c_in, s + 1)
        split(dot(rounded, agg_b[...]), q_own, q_out)
        row_scatter(Q_RS, q_out, q_in)
        split(dot(u_b[...], agg_b[...]), n_own, n_out)
        scatter(N_RS, n_out, n_in)
        n_all[me] = total(N_RS, n_own[me], n_in).astype(BF)
        gather(N_AG, n_all)

        @pl.when(leads)
        def _():
            q_own[slot] = total(Q_RS, q_own[slot], q_in)
            gathered(N_AG, n_all)

    @pl.when(jnp.logical_and(inner, leads))
    def _():
        b_own[slot] = total(B_RS, b_own[slot], b_in)
        q_own[slot] = total(Q_RS, q_own[slot], q_in)
        gathered(T_AG, t_all)

        @pl.when(s == 2)
        def _():
            c_all[slot] = cross_total(C_IN, c_in).astype(BF)

        @pl.when(s > 2)
        def _():
            arrived(C_ON, c_all.at[slot], me)

        held = c_all[slot]
        leaving = rotated(held.astype(F32), 0) + b_own[slot]
        c_out[...] = (leaving - dot(held, joined(t_all))).astype(BF)

        @pl.when(s < strips - 2)
        def _():
            hop(C_ON, c_out, c_all, s + 1)

        gathered(M_AG, m_all)
        q_own[slot] = q_own[slot] - dot(held, joined(m_all))

        @pl.when(is_turn)
        def _():
            turned = cross_total(R_RS, r_in)
            gathered(L_AG, l_all)
            d_all[slot] = (turned - dot(c_out[...], joined(l_all))).astype(BF)

        gathered(N_AG, n_all)

    between = jnp.logical_and(s > 0, s < strips - 1)

    @pl.when(jnp.logical_and(between, leads))
    def _():
        @pl.when(s < strips - 2)
        def _():
            arrived(D_ON, d_all.at[slot], me)

        held = d_all[slot]
        leaving = rotated(held.astype(F32), 2) + q_own[slot]
        d_out[...] = (leaving - dot(held, joined(n_all))).astype(BF)

        @pl.when(is_direct)
        def _():
            spread(D_ON, d_out, d_all, s - 1)

        @pl.when(s > 1)
        def _():
            hop(D_ON, d_out, d_all, s - 1)

        @pl.when(is_turn)
        def _():
            spread(C_ON, c_out, c_all, s + 1)

        @pl.when(s > 1)
        def _():
            share(C_SH, c_all)

        share(D_SH, d_all)

    @pl.when(is_last)
    def _():
        all_shared(C_ON, c_all)

    @pl.when(inner)
    def _():
        shared(C_SH, c_all)

    @pl.when(s > 1)
    def _():
        first_ref[0] = p[...] - dot(joined(c_all), u_f[...])

    @pl.when(is_last)
    def _():
        second_ref[0] = first_ref[0]

    @pl.when(is_first)
    def _():
        all_shared(D_ON, d_all)

    @pl.when(between)
    def _():
        shared(D_SH, d_all)

    @pl.when(s < strips - 1)
    def _():
        second_ref[0] = first_ref[0] - dot(joined(d_all), u_b[...])

    @pl.when(s < 2)
    def _():
        cross_row_scatter(C_IN, b_out, c_in, s + 1, sent)

    @pl.when(inner)
    def _():
        scatter(T_RS, t_out, t_in, sent)
        gather(T_AG, t_all, sent)
        scatter(M_RS, m_out, m_in, sent)
        gather(M_AG, m_all, sent)
        row_scatter(B_RS, b_out, b_in, sent)

    @pl.when(between)
    def _():
        scatter(N_RS, n_out, n_in, sent)
        gather(N_AG, n_all, sent)
        row_scatter(Q_RS, q_out, q_in, sent)

    @pl.when(is_turn)
    def _():
        gather(L_AG, l_all, sent)

    @pl.when(jnp.logical_and(between, leads))
    def _():
        share(C_SH, c_all, sent)
        share(D_SH, d_all, sent)

        @pl.when(is_turn)
        def _():
            spread(C_ON, c_out, c_all, s + 1, sent)

        @pl.when(jnp.logical_and(s > 1, s < strips - 2))
        def _():
            hop(C_ON, c_out, c_all, s + 1, sent)

        @pl.when(is_direct)
        def _():
            spread(D_ON, d_out, d_all, s - 1, sent)

        @pl.when(s > 1)
        def _():
            hop(D_ON, d_out, d_all, s - 1, sent)

    @pl.when(is_last)
    def _():
        cross_scatter(L_RS, m_out, l_in, s - 1, sent)
        cross_row_scatter(R_RS, q_out, r_in, s - 1, sent)


def body(strips, n, rhs, inverse, dis_fwd, agg_fwd, phase_fwd, gain_fwd, dis_back, agg_back, phase_back, gain_back):
    _, angles, unk = rhs.shape
    modes = agg_fwd.shape[2]
    width = 256 if unk % 256 == 0 else unk
    blocks = unk // width
    leaders = n // 2
    rows, part = angles // leaders, modes // n
    hbm = pl.BlockSpec(memory_space=pl.ANY)
    vmem = pl.BlockSpec(memory_space=pltpu.VMEM)
    out = pltpu.VMEM((1, angles, unk), F32)
    return pl.pallas_call(
        functools.partial(kernel, strips, n, width),
        out_shape=(out, out),
        in_specs=[hbm] * 10,
        out_specs=(vmem, vmem),
        scratch_shapes=[
            pltpu.VMEM((angles, unk), BF),
            pltpu.VMEM((modes, unk), BF),
            pltpu.VMEM((modes, unk), BF),
            pltpu.VMEM((blocks, unk, width), BF),
            pltpu.VMEM((unk, modes), BF),
            pltpu.VMEM((unk, modes), BF),
            pltpu.VMEM((angles, unk), F32),
            pltpu.VMEM((angles, unk), BF),
            pltpu.VMEM((modes, unk), BF),
            pltpu.VMEM((modes, unk), BF),
        ]
        + [pltpu.VMEM((n, part, modes), kind) for kind in (F32, BF, BF) * 3 + (BF,) * 5]
        + [
            pltpu.VMEM((count, rows, modes), kind)
            for count, kind in ((leaders, F32), (leaders, BF), (n, BF)) * 2 + ((n, BF),) * 2
        ]
        + [pltpu.VMEM((rows, modes), BF), pltpu.VMEM((leaders, rows, modes), BF)] * 2
        + [pltpu.VMEM((4, 1, modes // 2), F32)] * 2
        + [pltpu.SemaphoreType.DMA((9 + blocks,)), pltpu.SemaphoreType.DMA((KINDS, 2, n))],
        compiler_params=pltpu.CompilerParams(
            collective_id=0, has_side_effects=True, vmem_limit_bytes=60 * 1024 * 1024
        ),
    )(rhs, inverse, dis_fwd, agg_fwd, phase_fwd, gain_fwd, dis_back, agg_back, phase_back, gain_back)


def solution(mesh):
    strips, n = mesh.shape["strip"], mesh.shape["cross"]
    return jax.shard_map(
        functools.partial(body, strips, n),
        mesh=mesh,
        in_specs=(
            P("strip", None, "cross"),
            P("strip", "cross", None, None),
            P("strip", "cross", None, None),
            P("strip", "cross", None),
            P("strip", None),
            P("strip", None),
            P("strip", "cross", None, None),
            P("strip", "cross", None),
            P("strip", None),
            P("strip", None),
        ),
        out_specs=(P("strip", None, "cross"), P("strip", None, "cross")),
        check_vma=False,
    )
```

```python
import functools

import jax
import jax.numpy as jnp
from jax import lax
from jax.experimental import pallas as pl
from jax.experimental.pallas import tpu as pltpu
from jax.sharding import PartitionSpec as P

MESH = pl.DeviceIdType.MESH
BF = jnp.bfloat16
F32 = jnp.float32
KINDS = 16
(
    T_RS, T_AG, M_RS, M_AG, N_RS, N_AG, L_RS, L_AG,
    B_RS, Q_RS, R_RS, C_IN, C_ON, C_SH, D_ON, D_SH,
) = range(KINDS)


def dot(a, b):
    return jnp.dot(a, b, preferred_element_type=F32)


def kernel(
    strips, n, width,
    rhs, inverse, dis_fwd, agg_fwd, phase_fwd, gain_fwd, dis_back, agg_back, phase_back, gain_back,
    first_ref, second_ref,
    x_r, x_f, x_b, inv, agg_f, agg_b, p, z, u_f, u_b,
    t_own, t_out, t_in, m_own, m_out, m_in, n_own, n_out, n_in, l_in, t_all, m_all, n_all, l_all,
    b_own, b_out, b_in, q_own, q_out, q_in, r_in, c_in,
    c_out, c_all, d_out, d_all,
    turns, coef, load_sem, sems,
):
    s = lax.axis_index("strip")
    me = lax.axis_index("cross")
    is_first = s == 0
    is_direct = s == 1
    is_last = s == strips - 1
    is_turn = s == strips - 2
    inner = jnp.logical_and(s > 1, s < strips - 1)
    angles = rhs.shape[1]
    modes = agg_f.shape[1]
    half = modes // 2
    unk = p.shape[1]
    blocks = unk // width
    leaders = n // 2
    slot = me // 2
    follows = lax.rem(me, 2)
    leads = follows == 0

    barrier = pltpu.get_barrier_semaphore()

    def greet(strip, peer):
        pl.semaphore_signal(barrier, inc=1, device_id=(strip, peer), device_id_type=MESH)

    def others(fn):
        def step(j, carry):
            fn(lax.rem(me + j, n))
            return carry
        lax.fori_loop(1, n, step, 0)

    def everyone(fn):
        def step(j, carry):
            fn(lax.rem(me + j, n))
            return carry
        lax.fori_loop(0, n, step, 0)

    load_rhs = pltpu.make_async_copy(rhs.at[0], x_r, load_sem.at[0])
    load_dis = pltpu.make_async_copy(dis_fwd.at[0, 0], x_f, load_sem.at[1])
    load_agg = pltpu.make_async_copy(agg_fwd.at[0], agg_f, load_sem.at[2])
    load_dis_b = pltpu.make_async_copy(dis_back.at[0, 0], x_b, load_sem.at[3])
    load_agg_b = pltpu.make_async_copy(agg_back.at[0], agg_b, load_sem.at[4])
    inv_loads = [
        pltpu.make_async_copy(
            inverse.at[0, 0, :, pl.ds(j * width, width)], inv.at[j], load_sem.at[5 + j]
        )
        for j in range(blocks)
    ]
    turn_loads = [
        pltpu.make_async_copy(ref, turns.at[j], load_sem.at[5 + blocks + j])
        for j, ref in enumerate((phase_fwd, gain_fwd, phase_back, gain_back))
    ]
    @pl.when(is_first)
    def _():
        load_rhs.start()

    @pl.when(s > 0)
    def _():
        load_dis.start()

    for copy in inv_loads:
        copy.start()

    @pl.when(s > 0)
    def _():
        everyone(lambda peer: greet(s - 1, peer))

    @pl.when(s < strips - 1)
    def _():
        everyone(lambda peer: greet(s + 1, peer))

    others(lambda peer: greet(s, peer))

    @pl.when(s < strips - 1)
    def _():
        load_agg.start()

    @pl.when(s > 0)
    def _():
        load_agg_b.start()
        load_rhs.start()

    @pl.when(s < strips - 1)
    def _():
        load_dis_b.start()

    for copy in turn_loads:
        copy.start()

    def remote(kind, src, dst, strip, peer):
        return pltpu.make_async_remote_copy(
            src_ref=src,
            dst_ref=dst,
            send_sem=sems.at[kind, 0],
            recv_sem=sems.at[kind, 1],
            device_id=(strip, peer),
            device_id_type=MESH,
        )

    def other_leaders(fn):
        def step(j, carry):
            fn(2 * lax.rem(slot + j, leaders))
            return carry
        lax.fori_loop(1 - follows, leaders, step, 0)

    def every_leader(fn):
        def step(j, carry):
            fn(2 * lax.rem(slot + j, leaders))
            return carry
        lax.fori_loop(0, leaders, step, 0)

    def waiting(kind, ref):
        return pltpu.make_async_remote_copy(
            src_ref=ref,
            dst_ref=ref,
            send_sem=sems.at[kind, 0],
            recv_sem=sems.at[kind, 1],
            device_id=(s, lax.rem(me + 1, n)),
            device_id_type=MESH,
        )

    def arrived(kind, ref):
        waiting(kind, ref).wait_recv()

    def sent(kind, ref):
        waiting(kind, ref).wait_send()

    def by_role(act, kind, buf):
        @pl.when(leads)
        def _():
            act(kind, buf.at[pl.ds(0, leaders - 1)])

        @pl.when(follows == 1)
        def _():
            act(kind, buf.at[pl.ds(0, leaders)])

    def scatter(kind, out, into):
        others(lambda peer: remote(kind, out.at[peer], into.at[me], s, peer).start())

    def cross_scatter(kind, out, into, strip):
        everyone(lambda peer: remote(kind, out.at[peer], into.at[me], strip, peer).start())

    def row_scatter(kind, out, into):
        other_leaders(
            lambda peer: remote(kind, out.at[peer // 2], into.at[me], s, peer).start()
        )

    def cross_row_scatter(kind, out, into, strip):
        every_leader(
            lambda peer: remote(kind, out.at[peer // 2], into.at[me], strip, peer).start()
        )

    def gather(kind, buf):
        other_leaders(lambda peer: remote(kind, buf.at[me], buf.at[me], s, peer).start())

    def share(kind, buf):
        others(lambda peer: remote(kind, buf.at[slot], buf.at[slot], s, peer).start())

    def spread(kind, src, into, strip):
        everyone(lambda peer: remote(kind, src, into.at[slot], strip, peer).start())

    def hop(kind, src, into, strip):
        remote(kind, src, into.at[slot], strip, me).start()

    def total(kind, own, into):
        arrived(kind, into.at[pl.ds(0, n - 1)])
        value = own
        for j in range(1, n):
            value = value + into[lax.rem(me + j, n)].astype(F32)
        return value

    def cross_total(kind, into):
        arrived(kind, into)
        value = into[0].astype(F32)
        for j in range(1, n):
            value = value + into[j].astype(F32)
        return value

    def gathered(kind, buf):
        arrived(kind, buf.at[pl.ds(0, n - 1)])

    def shared(kind, buf):
        by_role(arrived, kind, buf)

    def split(value, own, out):
        pieces = own.shape[0]
        part = value.shape[0] // pieces
        for k in range(pieces):
            piece = value[k * part:(k + 1) * part]
            own[k] = piece
            out[k] = piece.astype(BF)

    def joined(buf):
        return jnp.concatenate([buf[k] for k in range(buf.shape[0])], axis=0)

    def rotated(value, at):
        real, imag = value[:, :half], value[:, half:]
        cosine, sine = coef[at], coef[at + 1]
        return jnp.concatenate(
            [cosine * real - sine * imag, sine * real + cosine * imag], axis=1
        )

    def columns(j):
        return slice(j * width, (j + 1) * width)

    cuts = sorted({0, min(2, blocks), min(4, blocks), blocks})
    groups = [range(a, b) for a, b in zip(cuts, cuts[1:])]

    def base_field(group):
        for j in group:
            product = dot(x_r[...], inv[j])
            p[:, columns(j)] = product
            z[:, columns(j)] = product.astype(BF)

    def back_matrix(group):
        for j in group:
            u_b[:, columns(j)] = dot(x_b[...], inv[j]).astype(BF)

    @pl.when(is_first)
    def _():
        load_rhs.wait()
        for group in groups:
            for j in group:
                inv_loads[j].wait()
            base_field(group)
        load_agg.wait()
        split(dot(z[...], agg_f[...]), b_own, b_out)

    @pl.when(s > 0)
    def _():
        load_dis.wait()
        for group in groups:
            for j in group:
                inv_loads[j].wait()
            for j in group:
                u_f[:, columns(j)] = dot(x_f[...], inv[j]).astype(BF)

    @pl.when(inner)
    def _():
        load_agg.wait()
        split(dot(u_f[...], agg_f[...]), t_own, t_out)

    @pl.when(s > 0)
    def _():
        load_agg_b.wait()

    @pl.when(is_last)
    def _():
        split(dot(u_f[...], agg_b[...]), m_own, m_out)

    greeted = (n - 1) + jnp.where(s > 0, n, 0) + jnp.where(s < strips - 1, n, 0)
    pl.semaphore_wait(barrier, greeted)

    for copy in turn_loads:
        copy.wait()

    def rotations():
        for at in (0, 2):
            coef[at] = jnp.cos(turns[at]) * turns[at + 1]
            coef[at + 1] = jnp.sin(turns[at]) * turns[at + 1]

    @pl.when(is_first)
    def _():
        cross_row_scatter(C_IN, b_out, c_in, s + 1)
        load_dis_b.wait()
        back_matrix(range(blocks))
        first_ref[0] = p[...]

    @pl.when(inner)
    def _():
        scatter(T_RS, t_out, t_in)
        split(dot(u_f[...], agg_b[...]), m_own, m_out)
        scatter(M_RS, m_out, m_in)
        load_dis_b.wait()
        back_matrix(range(blocks))
        split(dot(u_b[...], agg_b[...]), n_own, n_out)
        scatter(N_RS, n_out, n_in)
        load_rhs.wait()
        rotations()
        t_all[me] = total(T_RS, t_own[me], t_in).astype(BF)
        gather(T_AG, t_all)
        base_field(range(0, blocks // 2))
        m_all[me] = total(M_RS, m_own[me], m_in).astype(BF)
        gather(M_AG, m_all)

    @pl.when(is_turn)
    def _():
        l_all[me] = cross_total(L_RS, l_in).astype(BF)
        gather(L_AG, l_all)

    @pl.when(inner)
    def _():
        base_field(range(blocks // 2, blocks))
        split(dot(z[...], agg_f[...]), b_own, b_out)
        row_scatter(B_RS, b_out, b_in)
        split(dot(z[...], agg_b[...]), q_own, q_out)
        row_scatter(Q_RS, q_out, q_in)
        n_all[me] = total(N_RS, n_own[me], n_in).astype(BF)
        gather(N_AG, n_all)

    @pl.when(is_last)
    def _():
        cross_scatter(L_RS, m_out, l_in, s - 1)
        load_rhs.wait()
        base_field(range(blocks))
        split(dot(z[...], agg_b[...]), q_own, q_out)
        cross_row_scatter(R_RS, q_out, r_in, s - 1)

    @pl.when(is_direct)
    def _():
        load_rhs.wait()
        base_field(range(blocks))
        rotations()

        @pl.when(leads)
        def _():
            c_all[slot] = cross_total(C_IN, c_in).astype(BF)
            share(C_SH, c_all)

        load_dis_b.wait()
        back_matrix(range(blocks))
        load_agg.wait()
        shared(C_SH, c_all)
        first_ref[0] = p[...] - dot(joined(c_all), u_f[...])
        rounded = first_ref[0].astype(BF)
        split(dot(rounded, agg_f[...]), b_own, b_out)

        @pl.when(leads)
        def _():
            leaving = b_own[slot] + rotated(c_all[slot].astype(F32), 0)
            b_out[slot] = leaving.astype(BF)

        cross_row_scatter(C_IN, b_out, c_in, s + 1)
        split(dot(rounded, agg_b[...]), q_own, q_out)
        row_scatter(Q_RS, q_out, q_in)
        split(dot(u_b[...], agg_b[...]), n_own, n_out)
        scatter(N_RS, n_out, n_in)
        n_all[me] = total(N_RS, n_own[me], n_in).astype(BF)
        gather(N_AG, n_all)

        @pl.when(leads)
        def _():
            q_own[slot] = total(Q_RS, q_own[slot], q_in)
            gathered(N_AG, n_all)

    @pl.when(jnp.logical_and(inner, leads))
    def _():
        b_own[slot] = total(B_RS, b_own[slot], b_in)
        q_own[slot] = total(Q_RS, q_own[slot], q_in)
        gathered(T_AG, t_all)

        @pl.when(s == 2)
        def _():
            c_all[slot] = cross_total(C_IN, c_in).astype(BF)

        @pl.when(s > 2)
        def _():
            arrived(C_ON, c_all.at[slot])

        held = c_all[slot]
        leaving = rotated(held.astype(F32), 0) + b_own[slot]
        c_out[...] = (leaving - dot(held, joined(t_all))).astype(BF)

        @pl.when(s < strips - 2)
        def _():
            hop(C_ON, c_out, c_all, s + 1)

        gathered(M_AG, m_all)
        q_own[slot] = q_own[slot] - dot(held, joined(m_all))

        @pl.when(is_turn)
        def _():
            turned = cross_total(R_RS, r_in)
            gathered(L_AG, l_all)
            d_all[slot] = (turned - dot(c_out[...], joined(l_all))).astype(BF)

        gathered(N_AG, n_all)

    between = jnp.logical_and(s > 0, s < strips - 1)

    @pl.when(jnp.logical_and(between, leads))
    def _():
        @pl.when(s < strips - 2)
        def _():
            arrived(D_ON, d_all.at[slot])

        held = d_all[slot]
        leaving = rotated(held.astype(F32), 2) + q_own[slot]
        d_out[...] = (leaving - dot(held, joined(n_all))).astype(BF)

        @pl.when(is_direct)
        def _():
            spread(D_ON, d_out, d_all, s - 1)

        @pl.when(s > 1)
        def _():
            hop(D_ON, d_out, d_all, s - 1)
            sent(D_ON, d_out)

        @pl.when(is_turn)
        def _():
            spread(C_ON, c_out, c_all, s + 1)

        @pl.when(s > 1)
        def _():
            share(C_SH, c_all)

        share(D_SH, d_all)

    @pl.when(is_last)
    def _():
        arrived(C_ON, c_all)

    @pl.when(inner)
    def _():
        shared(C_SH, c_all)

    @pl.when(s > 1)
    def _():
        first_ref[0] = p[...] - dot(joined(c_all), u_f[...])

    @pl.when(is_last)
    def _():
        second_ref[0] = first_ref[0]

    @pl.when(is_first)
    def _():
        arrived(D_ON, d_all)

    @pl.when(between)
    def _():
        shared(D_SH, d_all)

    @pl.when(s < strips - 1)
    def _():
        second_ref[0] = first_ref[0] - dot(joined(d_all), u_b[...])

    @pl.when(s < 2)
    def _():
        sent(C_IN, b_out)

    @pl.when(inner)
    def _():
        sent(T_RS, t_out.at[pl.ds(0, n - 1)])
        sent(M_RS, m_out.at[pl.ds(0, n - 1)])
        by_role(sent, T_AG, t_all)
        by_role(sent, M_AG, m_all)
        by_role(sent, B_RS, b_out)

    @pl.when(between)
    def _():
        sent(N_RS, n_out.at[pl.ds(0, n - 1)])
        by_role(sent, N_AG, n_all)
        by_role(sent, Q_RS, q_out)

    @pl.when(is_turn)
    def _():
        by_role(sent, L_AG, l_all)

    @pl.when(jnp.logical_and(between, leads))
    def _():
        sent(C_SH, c_in.at[pl.ds(0, n - 1)])
        sent(D_SH, c_in.at[pl.ds(0, n - 1)])

        @pl.when(is_turn)
        def _():
            sent(C_ON, c_in)

        @pl.when(jnp.logical_and(s > 1, s < strips - 2))
        def _():
            sent(C_ON, c_out)

        @pl.when(is_direct)
        def _():
            sent(D_ON, c_in)

    @pl.when(is_last)
    def _():
        sent(L_RS, m_out)
        sent(R_RS, q_out)


def body(strips, n, rhs, inverse, dis_fwd, agg_fwd, phase_fwd, gain_fwd, dis_back, agg_back, phase_back, gain_back):
    _, angles, unk = rhs.shape
    modes = agg_fwd.shape[2]
    width = 256 if unk % 256 == 0 else unk
    blocks = unk // width
    leaders = n // 2
    rows, part = angles // leaders, modes // n
    hbm = pl.BlockSpec(memory_space=pl.ANY)
    vmem = pl.BlockSpec(memory_space=pltpu.VMEM)
    out = pltpu.VMEM((1, angles, unk), F32)
    return pl.pallas_call(
        functools.partial(kernel, strips, n, width),
        out_shape=(out, out),
        in_specs=[hbm] * 10,
        out_specs=(vmem, vmem),
        scratch_shapes=[
            pltpu.VMEM((angles, unk), BF),
            pltpu.VMEM((modes, unk), BF),
            pltpu.VMEM((modes, unk), BF),
            pltpu.VMEM((blocks, unk, width), BF),
            pltpu.VMEM((unk, modes), BF),
            pltpu.VMEM((unk, modes), BF),
            pltpu.VMEM((angles, unk), F32),
            pltpu.VMEM((angles, unk), BF),
            pltpu.VMEM((modes, unk), BF),
            pltpu.VMEM((modes, unk), BF),
        ]
        + [pltpu.VMEM((n, part, modes), kind) for kind in (F32, BF, BF) * 3 + (BF,) * 5]
        + [
            pltpu.VMEM((count, rows, modes), kind)
            for count, kind in ((leaders, F32), (leaders, BF), (n, BF)) * 2 + ((n, BF),) * 2
        ]
        + [pltpu.VMEM((rows, modes), BF), pltpu.VMEM((leaders, rows, modes), BF)] * 2
        + [pltpu.VMEM((4, 1, modes // 2), F32)] * 2
        + [pltpu.SemaphoreType.DMA((9 + blocks,)), pltpu.SemaphoreType.DMA((KINDS, 2))],
        compiler_params=pltpu.CompilerParams(
            collective_id=0, has_side_effects=True, vmem_limit_bytes=60 * 1024 * 1024
        ),
    )(rhs, inverse, dis_fwd, agg_fwd, phase_fwd, gain_fwd, dis_back, agg_back, phase_back, gain_back)


def solution(mesh):
    strips, n = mesh.shape["strip"], mesh.shape["cross"]
    return jax.shard_map(
        functools.partial(body, strips, n),
        mesh=mesh,
        in_specs=(
            P("strip", None, "cross"),
            P("strip", "cross", None, None),
            P("strip", "cross", None, None),
            P("strip", "cross", None),
            P("strip", None),
            P("strip", None),
            P("strip", "cross", None, None),
            P("strip", "cross", None),
            P("strip", None),
            P("strip", None),
        ),
        out_specs=(P("strip", None, "cross"), P("strip", None, "cross")),
        check_vma=False,
    )
```

```python
import functools

import jax
import jax.numpy as jnp
from jax import lax
from jax.experimental import pallas as pl
from jax.experimental.pallas import tpu as pltpu
from jax.sharding import PartitionSpec as P

MESH = pl.DeviceIdType.MESH
BF = jnp.bfloat16
F32 = jnp.float32
KINDS = 16
(
    T_RS, T_AG, M_RS, M_AG, N_RS, N_AG, L_RS, L_AG,
    B_RS, Q_RS, R_RS, C_IN, C_ON, C_SH, D_ON, D_SH,
) = range(KINDS)


def dot(a, b):
    return jnp.dot(a, b, preferred_element_type=F32)


def kernel(
    strips, n, width,
    rhs, inverse, dis_fwd, agg_fwd, phase_fwd, gain_fwd, dis_back, agg_back, phase_back, gain_back,
    p, cu, du,
    x_r, x_f, x_b, inv, agg_f, agg_b, z, u_f, u_b,
    t_own, t_out, t_in, m_own, m_out, m_in, n_own, n_out, n_in, l_in, t_all, m_all, n_all, l_all,
    b_own, b_out, b_in, q_own, q_out, q_in, r_in, c_in,
    c_out, c_all, d_out, d_all,
    turns, coef, load_sem, sems,
):
    s = lax.axis_index("strip")
    me = lax.axis_index("cross")
    is_first = s == 0
    is_direct = s == 1
    is_last = s == strips - 1
    is_turn = s == strips - 2
    inner = jnp.logical_and(s > 1, s < strips - 1)
    angles = rhs.shape[1]
    modes = agg_f.shape[1]
    half = modes // 2
    unk = p.shape[1]
    blocks = unk // width
    leaders = n // 2
    slot = me // 2
    follows = lax.rem(me, 2)
    leads = follows == 0

    barrier = pltpu.get_barrier_semaphore()

    def greet(strip, peer):
        pl.semaphore_signal(barrier, inc=1, device_id=(strip, peer), device_id_type=MESH)

    def others(fn):
        def step(j, carry):
            fn(lax.rem(me + j, n))
            return carry
        lax.fori_loop(1, n, step, 0)

    def everyone(fn):
        def step(j, carry):
            fn(lax.rem(me + j, n))
            return carry
        lax.fori_loop(0, n, step, 0)

    load_rhs = pltpu.make_async_copy(rhs.at[0], x_r, load_sem.at[0])
    load_dis = pltpu.make_async_copy(dis_fwd.at[0, 0], x_f, load_sem.at[1])
    load_agg = pltpu.make_async_copy(agg_fwd.at[0], agg_f, load_sem.at[2])
    load_dis_b = pltpu.make_async_copy(dis_back.at[0, 0], x_b, load_sem.at[3])
    load_agg_b = pltpu.make_async_copy(agg_back.at[0], agg_b, load_sem.at[4])
    inv_loads = [
        pltpu.make_async_copy(
            inverse.at[0, 0, :, pl.ds(j * width, width)], inv.at[j], load_sem.at[5 + j]
        )
        for j in range(blocks)
    ]
    turn_loads = [
        pltpu.make_async_copy(ref, turns.at[j], load_sem.at[5 + blocks + j])
        for j, ref in enumerate((phase_fwd, gain_fwd, phase_back, gain_back))
    ]
    @pl.when(is_first)
    def _():
        load_rhs.start()

    @pl.when(s > 0)
    def _():
        load_dis.start()

    for copy in inv_loads:
        copy.start()

    @pl.when(s > 0)
    def _():
        everyone(lambda peer: greet(s - 1, peer))

    @pl.when(s < strips - 1)
    def _():
        everyone(lambda peer: greet(s + 1, peer))

    others(lambda peer: greet(s, peer))

    @pl.when(s < strips - 1)
    def _():
        load_agg.start()

    @pl.when(s > 0)
    def _():
        load_agg_b.start()
        load_rhs.start()

    @pl.when(s < strips - 1)
    def _():
        load_dis_b.start()

    for copy in turn_loads:
        copy.start()

    def remote(kind, src, dst, strip, peer):
        return pltpu.make_async_remote_copy(
            src_ref=src,
            dst_ref=dst,
            send_sem=sems.at[kind, 0],
            recv_sem=sems.at[kind, 1],
            device_id=(strip, peer),
            device_id_type=MESH,
        )

    def other_leaders(fn):
        def step(j, carry):
            fn(2 * lax.rem(slot + j, leaders))
            return carry
        lax.fori_loop(1 - follows, leaders, step, 0)

    def every_leader(fn):
        def step(j, carry):
            fn(2 * lax.rem(slot + j, leaders))
            return carry
        lax.fori_loop(0, leaders, step, 0)

    def waiting(kind, ref):
        return pltpu.make_async_remote_copy(
            src_ref=ref,
            dst_ref=ref,
            send_sem=sems.at[kind, 0],
            recv_sem=sems.at[kind, 1],
            device_id=(s, lax.rem(me + 1, n)),
            device_id_type=MESH,
        )

    def arrived(kind, ref):
        waiting(kind, ref).wait_recv()

    def sent(kind, ref):
        waiting(kind, ref).wait_send()

    def by_role(act, kind, buf):
        @pl.when(leads)
        def _():
            act(kind, buf.at[pl.ds(0, leaders - 1)])

        @pl.when(follows == 1)
        def _():
            act(kind, buf.at[pl.ds(0, leaders)])

    def scatter(kind, out, into):
        others(lambda peer: remote(kind, out.at[peer], into.at[me], s, peer).start())

    def cross_scatter(kind, out, into, strip):
        everyone(lambda peer: remote(kind, out.at[peer], into.at[me], strip, peer).start())

    def row_scatter(kind, out, into):
        other_leaders(
            lambda peer: remote(kind, out.at[peer // 2], into.at[me], s, peer).start()
        )

    def cross_row_scatter(kind, out, into, strip):
        every_leader(
            lambda peer: remote(kind, out.at[peer // 2], into.at[me], strip, peer).start()
        )

    def gather(kind, buf):
        other_leaders(lambda peer: remote(kind, buf.at[me], buf.at[me], s, peer).start())

    def share(kind, buf):
        others(lambda peer: remote(kind, buf.at[slot], buf.at[slot], s, peer).start())

    def spread(kind, src, into, strip):
        everyone(lambda peer: remote(kind, src, into.at[slot], strip, peer).start())

    def hop(kind, src, into, strip):
        remote(kind, src, into.at[slot], strip, me).start()

    def total(kind, own, into):
        arrived(kind, into.at[pl.ds(0, n - 1)])
        value = own
        for j in range(1, n):
            value = value + into[lax.rem(me + j, n)].astype(F32)
        return value

    def cross_total(kind, into):
        arrived(kind, into)
        value = into[0].astype(F32)
        for j in range(1, n):
            value = value + into[j].astype(F32)
        return value

    def gathered(kind, buf):
        arrived(kind, buf.at[pl.ds(0, n - 1)])

    def shared(kind, buf):
        by_role(arrived, kind, buf)

    def split(value, own, out):
        pieces = own.shape[0]
        part = value.shape[0] // pieces
        for k in range(pieces):
            piece = value[k * part:(k + 1) * part]
            own[k] = piece
            out[k] = piece.astype(BF)

    def joined(buf):
        return jnp.concatenate([buf[k] for k in range(buf.shape[0])], axis=0)

    def rotated(value, at):
        real, imag = value[:, :half], value[:, half:]
        cosine, sine = coef[at], coef[at + 1]
        return jnp.concatenate(
            [cosine * real - sine * imag, sine * real + cosine * imag], axis=1
        )

    def columns(j):
        return slice(j * width, (j + 1) * width)

    cuts = sorted({0, min(2, blocks), min(4, blocks), blocks})
    groups = [range(a, b) for a, b in zip(cuts, cuts[1:])]

    def base_field(group):
        for j in group:
            product = dot(x_r[...], inv[j])
            p[:, columns(j)] = product
            z[:, columns(j)] = product.astype(BF)

    def back_matrix(group):
        for j in group:
            u_b[:, columns(j)] = dot(x_b[...], inv[j]).astype(BF)

    @pl.when(is_first)
    def _():
        load_rhs.wait()
        for group in groups:
            for j in group:
                inv_loads[j].wait()
            base_field(group)
        load_agg.wait()
        split(dot(z[...], agg_f[...]), b_own, b_out)

    @pl.when(s > 0)
    def _():
        load_dis.wait()
        for group in groups:
            for j in group:
                inv_loads[j].wait()
            for j in group:
                u_f[:, columns(j)] = dot(x_f[...], inv[j]).astype(BF)

    @pl.when(inner)
    def _():
        load_agg.wait()
        split(dot(u_f[...], agg_f[...]), t_own, t_out)

    @pl.when(s > 0)
    def _():
        load_agg_b.wait()

    @pl.when(is_last)
    def _():
        split(dot(u_f[...], agg_b[...]), m_own, m_out)

    greeted = (n - 1) + jnp.where(s > 0, n, 0) + jnp.where(s < strips - 1, n, 0)
    pl.semaphore_wait(barrier, greeted)

    for copy in turn_loads:
        copy.wait()

    def rotations():
        for at in (0, 2):
            coef[at] = jnp.cos(turns[at]) * turns[at + 1]
            coef[at + 1] = jnp.sin(turns[at]) * turns[at + 1]

    @pl.when(is_first)
    def _():
        cross_row_scatter(C_IN, b_out, c_in, s + 1)
        load_dis_b.wait()
        back_matrix(range(blocks))
        cu[...] = jnp.zeros_like(cu)

    @pl.when(inner)
    def _():
        scatter(T_RS, t_out, t_in)
        split(dot(u_f[...], agg_b[...]), m_own, m_out)
        scatter(M_RS, m_out, m_in)
        load_dis_b.wait()
        back_matrix(range(blocks))
        split(dot(u_b[...], agg_b[...]), n_own, n_out)
        scatter(N_RS, n_out, n_in)
        load_rhs.wait()
        base_field(range(blocks))
        rotations()
        t_all[me] = total(T_RS, t_own[me], t_in).astype(BF)
        gather(T_AG, t_all)
        split(dot(z[...], agg_f[...]), b_own, b_out)
        row_scatter(B_RS, b_out, b_in)
        split(dot(z[...], agg_b[...]), q_own, q_out)
        row_scatter(Q_RS, q_out, q_in)
        m_all[me] = total(M_RS, m_own[me], m_in).astype(BF)
        gather(M_AG, m_all)

    @pl.when(is_turn)
    def _():
        l_all[me] = cross_total(L_RS, l_in).astype(BF)
        gather(L_AG, l_all)

    @pl.when(inner)
    def _():
        n_all[me] = total(N_RS, n_own[me], n_in).astype(BF)
        gather(N_AG, n_all)

    @pl.when(is_last)
    def _():
        cross_scatter(L_RS, m_out, l_in, s - 1)
        load_rhs.wait()
        base_field(range(blocks))
        split(dot(z[...], agg_b[...]), q_own, q_out)
        cross_row_scatter(R_RS, q_out, r_in, s - 1)
        du[...] = jnp.zeros_like(du)

    @pl.when(is_direct)
    def _():
        load_rhs.wait()
        base_field(range(blocks))
        rotations()

        @pl.when(leads)
        def _():
            c_all[slot] = cross_total(C_IN, c_in).astype(BF)
            share(C_SH, c_all)

        load_dis_b.wait()
        back_matrix(range(blocks))
        load_agg.wait()
        shared(C_SH, c_all)
        cu[...] = dot(joined(c_all), u_f[...])
        rounded = (p[...] - cu[...]).astype(BF)
        split(dot(rounded, agg_f[...]), b_own, b_out)

        @pl.when(leads)
        def _():
            leaving = b_own[slot] + rotated(c_all[slot].astype(F32), 0)
            b_out[slot] = leaving.astype(BF)

        cross_row_scatter(C_IN, b_out, c_in, s + 1)
        split(dot(rounded, agg_b[...]), q_own, q_out)
        row_scatter(Q_RS, q_out, q_in)
        split(dot(u_b[...], agg_b[...]), n_own, n_out)
        scatter(N_RS, n_out, n_in)
        n_all[me] = total(N_RS, n_own[me], n_in).astype(BF)
        gather(N_AG, n_all)

        @pl.when(leads)
        def _():
            q_own[slot] = total(Q_RS, q_own[slot], q_in)
            gathered(N_AG, n_all)

    @pl.when(jnp.logical_and(inner, leads))
    def _():
        b_own[slot] = total(B_RS, b_own[slot], b_in)
        q_own[slot] = total(Q_RS, q_own[slot], q_in)
        gathered(T_AG, t_all)

        @pl.when(s == 2)
        def _():
            c_all[slot] = cross_total(C_IN, c_in).astype(BF)

        @pl.when(s > 2)
        def _():
            arrived(C_ON, c_all.at[slot])

        held = c_all[slot]
        leaving = rotated(held.astype(F32), 0) + b_own[slot]
        c_out[...] = (leaving - dot(held, joined(t_all))).astype(BF)

        @pl.when(s < strips - 2)
        def _():
            hop(C_ON, c_out, c_all, s + 1)

        gathered(M_AG, m_all)
        q_own[slot] = q_own[slot] - dot(held, joined(m_all))

        @pl.when(is_turn)
        def _():
            turned = cross_total(R_RS, r_in)
            gathered(L_AG, l_all)
            d_all[slot] = (turned - dot(c_out[...], joined(l_all))).astype(BF)

        gathered(N_AG, n_all)

    between = jnp.logical_and(s > 0, s < strips - 1)

    @pl.when(jnp.logical_and(between, leads))
    def _():
        @pl.when(s < strips - 2)
        def _():
            arrived(D_ON, d_all.at[slot])

        held = d_all[slot]
        leaving = rotated(held.astype(F32), 2) + q_own[slot]
        d_out[...] = (leaving - dot(held, joined(n_all))).astype(BF)

        @pl.when(is_direct)
        def _():
            spread(D_ON, d_out, d_all, s - 1)

        @pl.when(s > 1)
        def _():
            hop(D_ON, d_out, d_all, s - 1)
            sent(D_ON, d_out)

        @pl.when(is_turn)
        def _():
            spread(C_ON, c_out, c_all, s + 1)

        @pl.when(s > 1)
        def _():
            share(C_SH, c_all)

        share(D_SH, d_all)

    @pl.when(is_last)
    def _():
        arrived(C_ON, c_all)

    @pl.when(inner)
    def _():
        shared(C_SH, c_all)

    @pl.when(s > 1)
    def _():
        cu[...] = dot(joined(c_all), u_f[...])

    @pl.when(is_first)
    def _():
        arrived(D_ON, d_all)

    @pl.when(between)
    def _():
        shared(D_SH, d_all)

    @pl.when(s < strips - 1)
    def _():
        du[...] = dot(joined(d_all), u_b[...])

    @pl.when(s < 2)
    def _():
        sent(C_IN, b_out)

    @pl.when(inner)
    def _():
        sent(T_RS, t_out.at[pl.ds(0, n - 1)])
        sent(M_RS, m_out.at[pl.ds(0, n - 1)])
        by_role(sent, T_AG, t_all)
        by_role(sent, M_AG, m_all)
        by_role(sent, B_RS, b_out)

    @pl.when(between)
    def _():
        sent(N_RS, n_out.at[pl.ds(0, n - 1)])
        by_role(sent, N_AG, n_all)
        by_role(sent, Q_RS, q_out)

    @pl.when(is_turn)
    def _():
        by_role(sent, L_AG, l_all)

    @pl.when(jnp.logical_and(between, leads))
    def _():
        sent(C_SH, c_in.at[pl.ds(0, n - 1)])
        sent(D_SH, c_in.at[pl.ds(0, n - 1)])

        @pl.when(is_turn)
        def _():
            sent(C_ON, c_in)

        @pl.when(jnp.logical_and(s > 1, s < strips - 2))
        def _():
            sent(C_ON, c_out)

        @pl.when(is_direct)
        def _():
            sent(D_ON, c_in)

    @pl.when(is_last)
    def _():
        sent(L_RS, m_out)
        sent(R_RS, q_out)


def body(strips, n, rhs, inverse, dis_fwd, agg_fwd, phase_fwd, gain_fwd, dis_back, agg_back, phase_back, gain_back):
    _, angles, unk = rhs.shape
    modes = agg_fwd.shape[2]
    width = 256 if unk % 256 == 0 else unk
    blocks = unk // width
    leaders = n // 2
    rows, part = angles // leaders, modes // n
    hbm = pl.BlockSpec(memory_space=pl.ANY)
    vmem = pl.BlockSpec(memory_space=pltpu.VMEM)
    out = pltpu.VMEM((angles, unk), F32)
    base, cu, du = pl.pallas_call(
        functools.partial(kernel, strips, n, width),
        out_shape=(out,) * 3,
        in_specs=[hbm] * 10,
        out_specs=(vmem,) * 3,
        scratch_shapes=[
            pltpu.VMEM((angles, unk), BF),
            pltpu.VMEM((modes, unk), BF),
            pltpu.VMEM((modes, unk), BF),
            pltpu.VMEM((blocks, unk, width), BF),
            pltpu.VMEM((unk, modes), BF),
            pltpu.VMEM((unk, modes), BF),
            pltpu.VMEM((angles, unk), BF),
            pltpu.VMEM((modes, unk), BF),
            pltpu.VMEM((modes, unk), BF),
        ]
        + [pltpu.VMEM((n, part, modes), kind) for kind in (F32, BF, BF) * 3 + (BF,) * 5]
        + [
            pltpu.VMEM((count, rows, modes), kind)
            for count, kind in ((leaders, F32), (leaders, BF), (n, BF)) * 2 + ((n, BF),) * 2
        ]
        + [pltpu.VMEM((rows, modes), BF), pltpu.VMEM((leaders, rows, modes), BF)] * 2
        + [pltpu.VMEM((4, 1, modes // 2), F32)] * 2
        + [pltpu.SemaphoreType.DMA((9 + blocks,)), pltpu.SemaphoreType.DMA((KINDS, 2))],
        compiler_params=pltpu.CompilerParams(
            collective_id=0, has_side_effects=True, vmem_limit_bytes=60 * 1024 * 1024
        ),
    )(rhs, inverse, dis_fwd, agg_fwd, phase_fwd, gain_fwd, dis_back, agg_back, phase_back, gain_back)
    first = base - cu
    return first[None], (first - du)[None]


def solution(mesh):
    strips, n = mesh.shape["strip"], mesh.shape["cross"]
    return jax.shard_map(
        functools.partial(body, strips, n),
        mesh=mesh,
        in_specs=(
            P("strip", None, "cross"),
            P("strip", "cross", None, None),
            P("strip", "cross", None, None),
            P("strip", "cross", None),
            P("strip", None),
            P("strip", None),
            P("strip", "cross", None, None),
            P("strip", "cross", None),
            P("strip", None),
            P("strip", None),
        ),
        out_specs=(P("strip", None, "cross"), P("strip", None, "cross")),
        check_vma=False,
    )
```

```python
import functools

import jax
import jax.numpy as jnp
from jax import lax
from jax.experimental import pallas as pl
from jax.experimental.pallas import tpu as pltpu
from jax.sharding import PartitionSpec as P

MESH = pl.DeviceIdType.MESH
BF = jnp.bfloat16
F32 = jnp.float32
KINDS = 18
(
    T_PR, M_PR, N_PR, T_RS, T_AG, M_RS, M_AG, N_RS, N_AG, L_AG,
    B_RS, Q_RS, R_RS, C_IN, C_ON, C_SH, D_ON, D_SH,
) = range(KINDS)


def dot(a, b):
    return jnp.dot(a, b, preferred_element_type=F32)


def kernel(
    strips, n, width,
    rhs, inverse, dis_fwd, agg_fwd, phase_fwd, gain_fwd, dis_back, agg_back, phase_back, gain_back,
    p, cu, du,
    x_r, x_f, x_b, inv, agg_f, agg_b, z, u_f, u_b,
    t_own, m_own, n_own, t_out, m_out, n_out, t_pair, m_pair, n_pair, t_in, m_in, n_in,
    t_all, m_all, n_all, l_all,
    b_own, b_out, b_in, q_own, q_out, q_in, r_in, c_in,
    c_out, c_all, d_out, d_all,
    turns, coef, load_sem, sems,
):
    s = lax.axis_index("strip")
    me = lax.axis_index("cross")
    is_first = s == 0
    is_direct = s == 1
    is_last = s == strips - 1
    is_turn = s == strips - 2
    inner = jnp.logical_and(s > 1, s < strips - 1)
    angles = rhs.shape[1]
    modes = agg_f.shape[1]
    half = modes // 2
    unk = p.shape[1]
    blocks = unk // width
    leaders = n // 2
    slot = me // 2
    follows = lax.rem(me, 2)
    leads = follows == 0

    barrier = pltpu.get_barrier_semaphore()

    def greet(strip, peer):
        pl.semaphore_signal(barrier, inc=1, device_id=(strip, peer), device_id_type=MESH)

    def others(fn):
        def step(j, carry):
            fn(lax.rem(me + j, n))
            return carry
        lax.fori_loop(1, n, step, 0)

    def everyone(fn):
        def step(j, carry):
            fn(lax.rem(me + j, n))
            return carry
        lax.fori_loop(0, n, step, 0)

    load_rhs = pltpu.make_async_copy(rhs.at[0], x_r, load_sem.at[0])
    load_dis = pltpu.make_async_copy(dis_fwd.at[0, 0], x_f, load_sem.at[1])
    load_agg = pltpu.make_async_copy(agg_fwd.at[0], agg_f, load_sem.at[2])
    load_dis_b = pltpu.make_async_copy(dis_back.at[0, 0], x_b, load_sem.at[3])
    load_agg_b = pltpu.make_async_copy(agg_back.at[0], agg_b, load_sem.at[4])
    inv_loads = [
        pltpu.make_async_copy(
            inverse.at[0, 0, :, pl.ds(j * width, width)], inv.at[j], load_sem.at[5 + j]
        )
        for j in range(blocks)
    ]
    turn_loads = [
        pltpu.make_async_copy(ref, turns.at[j], load_sem.at[5 + blocks + j])
        for j, ref in enumerate((phase_fwd, gain_fwd, phase_back, gain_back))
    ]
    @pl.when(is_first)
    def _():
        load_rhs.start()

    @pl.when(s > 0)
    def _():
        load_dis.start()

    for copy in inv_loads:
        copy.start()

    @pl.when(s > 0)
    def _():
        everyone(lambda peer: greet(s - 1, peer))

    @pl.when(s < strips - 1)
    def _():
        everyone(lambda peer: greet(s + 1, peer))

    others(lambda peer: greet(s, peer))

    @pl.when(s < strips - 1)
    def _():
        load_agg.start()

    @pl.when(s > 0)
    def _():
        load_agg_b.start()
        load_rhs.start()

    @pl.when(s < strips - 1)
    def _():
        load_dis_b.start()

    for copy in turn_loads:
        copy.start()

    def remote(kind, src, dst, strip, peer):
        return pltpu.make_async_remote_copy(
            src_ref=src,
            dst_ref=dst,
            send_sem=sems.at[kind, 0],
            recv_sem=sems.at[kind, 1],
            device_id=(strip, peer),
            device_id_type=MESH,
        )

    def other_leaders(fn):
        def step(j, carry):
            fn(2 * lax.rem(slot + j, leaders))
            return carry
        lax.fori_loop(1 - follows, leaders, step, 0)

    def every_leader(fn):
        def step(j, carry):
            fn(2 * lax.rem(slot + j, leaders))
            return carry
        lax.fori_loop(0, leaders, step, 0)

    def waiting(kind, ref):
        return pltpu.make_async_remote_copy(
            src_ref=ref,
            dst_ref=ref,
            send_sem=sems.at[kind, 0],
            recv_sem=sems.at[kind, 1],
            device_id=(s, lax.rem(me + 1, n)),
            device_id_type=MESH,
        )

    def arrived(kind, ref):
        waiting(kind, ref).wait_recv()

    def sent(kind, ref):
        waiting(kind, ref).wait_send()

    def by_role(act, kind, buf):
        @pl.when(leads)
        def _():
            act(kind, buf.at[pl.ds(0, leaders - 1)])

        @pl.when(follows == 1)
        def _():
            act(kind, buf.at[pl.ds(0, leaders)])

    def split_pairs(value, own, out):
        part = value.shape[0] // n
        for k in range(n):
            piece = value[k * part:(k + 1) * part]
            own[k % 2, k // 2] = piece
            out[k % 2, k // 2] = piece.astype(BF)

    def pair_send(kind, out, pair):
        remote(kind, out.at[1 - follows], pair, s, me + 1 - 2 * follows).start()

    def pair_scatter(pair_kind, kind, own, out, pair, into):
        arrived(pair_kind, pair)
        value = own[follows] + pair[...].astype(F32)
        own[follows] = value
        out[follows] = value.astype(BF)

        def step(j, carry):
            at = lax.rem(slot + j, leaders)
            remote(kind, out.at[follows, at], into.at[slot], s, 2 * at + follows).start()
            return carry

        lax.fori_loop(1, leaders, step, 0)

    def pair_total(kind, own, into):
        arrived(kind, into.at[pl.ds(0, leaders - 1)])
        value = own[follows, slot]
        for j in range(1, leaders):
            value = value + into[lax.rem(slot + j, leaders)].astype(F32)
        return value

    def pair_sent(pair_kind, kind, pair):
        sent(pair_kind, pair)
        sent(kind, pair.at[pl.ds(0, leaders - 1)])

    def row_scatter(kind, out, into):
        other_leaders(
            lambda peer: remote(kind, out.at[peer // 2], into.at[me], s, peer).start()
        )

    def cross_row_scatter(kind, out, into, strip):
        every_leader(
            lambda peer: remote(kind, out.at[peer // 2], into.at[me], strip, peer).start()
        )

    def gather(kind, buf):
        other_leaders(lambda peer: remote(kind, buf.at[me], buf.at[me], s, peer).start())

    def share(kind, buf):
        others(lambda peer: remote(kind, buf.at[slot], buf.at[slot], s, peer).start())

    def spread(kind, src, into, strip):
        everyone(lambda peer: remote(kind, src, into.at[slot], strip, peer).start())

    def hop(kind, src, into, strip):
        remote(kind, src, into.at[slot], strip, me).start()

    def total(kind, own, into):
        arrived(kind, into.at[pl.ds(0, n - 1)])
        value = own
        for j in range(1, n):
            value = value + into[lax.rem(me + j, n)].astype(F32)
        return value

    def cross_total(kind, into):
        arrived(kind, into)
        value = into[0].astype(F32)
        for j in range(1, n):
            value = value + into[j].astype(F32)
        return value

    def gathered(kind, buf):
        arrived(kind, buf.at[pl.ds(0, n - 1)])

    def shared(kind, buf):
        by_role(arrived, kind, buf)

    def split(value, own, out):
        pieces = own.shape[0]
        part = value.shape[0] // pieces
        for k in range(pieces):
            piece = value[k * part:(k + 1) * part]
            own[k] = piece
            out[k] = piece.astype(BF)

    def joined(buf):
        return jnp.concatenate([buf[k] for k in range(buf.shape[0])], axis=0)

    def rotated(value, at):
        real, imag = value[:, :half], value[:, half:]
        cosine, sine = coef[at], coef[at + 1]
        return jnp.concatenate(
            [cosine * real - sine * imag, sine * real + cosine * imag], axis=1
        )

    def columns(j):
        return slice(j * width, (j + 1) * width)

    cuts = sorted({0, min(2, blocks), min(4, blocks), blocks})
    groups = [range(a, b) for a, b in zip(cuts, cuts[1:])]

    def base_field(group):
        for j in group:
            product = dot(x_r[...], inv[j])
            p[:, columns(j)] = product
            z[:, columns(j)] = product.astype(BF)

    def back_matrix(group):
        for j in group:
            u_b[:, columns(j)] = dot(x_b[...], inv[j]).astype(BF)

    @pl.when(is_first)
    def _():
        load_rhs.wait()
        for group in groups:
            for j in group:
                inv_loads[j].wait()
            base_field(group)
        load_agg.wait()
        split(dot(z[...], agg_f[...]), b_own, b_out)

    @pl.when(s > 0)
    def _():
        load_dis.wait()
        for group in groups:
            for j in group:
                inv_loads[j].wait()
            for j in group:
                u_f[:, columns(j)] = dot(x_f[...], inv[j]).astype(BF)

    @pl.when(inner)
    def _():
        load_agg.wait()
        split_pairs(dot(u_f[...], agg_f[...]), t_own, t_out)

    @pl.when(s > 0)
    def _():
        load_agg_b.wait()

    @pl.when(is_last)
    def _():
        split_pairs(dot(u_f[...], agg_b[...]), m_own, m_out)

    greeted = (n - 1) + jnp.where(s > 0, n, 0) + jnp.where(s < strips - 1, n, 0)
    pl.semaphore_wait(barrier, greeted)

    for copy in turn_loads:
        copy.wait()

    def rotations():
        for at in (0, 2):
            coef[at] = jnp.cos(turns[at]) * turns[at + 1]
            coef[at + 1] = jnp.sin(turns[at]) * turns[at + 1]

    @pl.when(is_first)
    def _():
        cross_row_scatter(C_IN, b_out, c_in, s + 1)
        load_dis_b.wait()
        back_matrix(range(blocks))
        cu[...] = jnp.zeros_like(cu)

    @pl.when(inner)
    def _():
        pair_send(T_PR, t_out, t_pair)
        split_pairs(dot(u_f[...], agg_b[...]), m_own, m_out)
        pair_send(M_PR, m_out, m_pair)
        load_dis_b.wait()
        back_matrix(range(0, blocks // 2))
        pair_scatter(T_PR, T_RS, t_own, t_out, t_pair, t_in)
        pair_scatter(M_PR, M_RS, m_own, m_out, m_pair, m_in)
        back_matrix(range(blocks // 2, blocks))
        split_pairs(dot(u_b[...], agg_b[...]), n_own, n_out)
        pair_send(N_PR, n_out, n_pair)
        load_rhs.wait()
        base_field(range(0, (blocks + 1) // 2))
        pair_scatter(N_PR, N_RS, n_own, n_out, n_pair, n_in)
        base_field(range((blocks + 1) // 2, blocks))
        rotations()
        t_all[me] = pair_total(T_RS, t_own, t_in).astype(BF)
        gather(T_AG, t_all)
        split(dot(z[...], agg_f[...]), b_own, b_out)
        row_scatter(B_RS, b_out, b_in)
        split(dot(z[...], agg_b[...]), q_own, q_out)
        row_scatter(Q_RS, q_out, q_in)
        m_all[me] = pair_total(M_RS, m_own, m_in).astype(BF)
        gather(M_AG, m_all)
        n_all[me] = pair_total(N_RS, n_own, n_in).astype(BF)
        gather(N_AG, n_all)

    @pl.when(is_last)
    def _():
        pair_send(M_PR, m_out, m_pair)
        load_rhs.wait()
        base_field(range(0, (blocks + 1) // 2))
        pair_scatter(M_PR, M_RS, m_own, m_out, m_pair, m_in)
        base_field(range((blocks + 1) // 2, blocks))
        split(dot(z[...], agg_b[...]), q_own, q_out)
        cross_row_scatter(R_RS, q_out, r_in, s - 1)
        du[...] = jnp.zeros_like(du)
        m_all[me] = pair_total(M_RS, m_own, m_in).astype(BF)
        every_leader(
            lambda peer: remote(L_AG, m_all.at[me], l_all.at[me], s - 1, peer).start()
        )

    @pl.when(is_direct)
    def _():
        load_rhs.wait()
        base_field(range(blocks))
        rotations()

        @pl.when(leads)
        def _():
            c_all[slot] = cross_total(C_IN, c_in).astype(BF)
            share(C_SH, c_all)

        load_dis_b.wait()
        back_matrix(range(blocks))
        split_pairs(dot(u_b[...], agg_b[...]), n_own, n_out)
        pair_send(N_PR, n_out, n_pair)
        load_agg.wait()
        shared(C_SH, c_all)
        cu[...] = dot(joined(c_all), u_f[...])
        rounded = (p[...] - cu[...]).astype(BF)
        split(dot(rounded, agg_f[...]), b_own, b_out)

        @pl.when(leads)
        def _():
            leaving = b_own[slot] + rotated(c_all[slot].astype(F32), 0)
            b_out[slot] = leaving.astype(BF)

        cross_row_scatter(C_IN, b_out, c_in, s + 1)
        split(dot(rounded, agg_b[...]), q_own, q_out)
        row_scatter(Q_RS, q_out, q_in)
        pair_scatter(N_PR, N_RS, n_own, n_out, n_pair, n_in)
        n_all[me] = pair_total(N_RS, n_own, n_in).astype(BF)
        gather(N_AG, n_all)

        @pl.when(leads)
        def _():
            q_own[slot] = total(Q_RS, q_own[slot], q_in)
            gathered(N_AG, n_all)

    @pl.when(jnp.logical_and(inner, leads))
    def _():
        b_own[slot] = total(B_RS, b_own[slot], b_in)
        q_own[slot] = total(Q_RS, q_own[slot], q_in)
        gathered(T_AG, t_all)

        @pl.when(s == 2)
        def _():
            c_all[slot] = cross_total(C_IN, c_in).astype(BF)

        @pl.when(s > 2)
        def _():
            arrived(C_ON, c_all.at[slot])

        held = c_all[slot]
        leaving = rotated(held.astype(F32), 0) + b_own[slot]
        c_out[...] = (leaving - dot(held, joined(t_all))).astype(BF)

        @pl.when(s < strips - 2)
        def _():
            hop(C_ON, c_out, c_all, s + 1)

        gathered(M_AG, m_all)
        q_own[slot] = q_own[slot] - dot(held, joined(m_all))

        @pl.when(is_turn)
        def _():
            turned = cross_total(R_RS, r_in)
            arrived(L_AG, l_all)
            d_all[slot] = (turned - dot(c_out[...], joined(l_all))).astype(BF)

        gathered(N_AG, n_all)

    between = jnp.logical_and(s > 0, s < strips - 1)

    @pl.when(jnp.logical_and(between, leads))
    def _():
        @pl.when(s < strips - 2)
        def _():
            arrived(D_ON, d_all.at[slot])

        held = d_all[slot]
        leaving = rotated(held.astype(F32), 2) + q_own[slot]
        d_out[...] = (leaving - dot(held, joined(n_all))).astype(BF)

        @pl.when(is_direct)
        def _():
            spread(D_ON, d_out, d_all, s - 1)

        @pl.when(s > 1)
        def _():
            hop(D_ON, d_out, d_all, s - 1)
            sent(D_ON, d_out)

        @pl.when(is_turn)
        def _():
            spread(C_ON, c_out, c_all, s + 1)

        @pl.when(s > 1)
        def _():
            share(C_SH, c_all)

        share(D_SH, d_all)

    @pl.when(is_last)
    def _():
        arrived(C_ON, c_all)

    @pl.when(inner)
    def _():
        shared(C_SH, c_all)

    @pl.when(s > 1)
    def _():
        cu[...] = dot(joined(c_all), u_f[...])

    @pl.when(is_first)
    def _():
        arrived(D_ON, d_all)

    @pl.when(between)
    def _():
        shared(D_SH, d_all)

    @pl.when(s < strips - 1)
    def _():
        du[...] = dot(joined(d_all), u_b[...])

    @pl.when(s < 2)
    def _():
        sent(C_IN, b_out)

    @pl.when(inner)
    def _():
        pair_sent(T_PR, T_RS, t_pair)
        pair_sent(M_PR, M_RS, m_pair)
        by_role(sent, T_AG, t_all)
        by_role(sent, M_AG, m_all)
        by_role(sent, B_RS, b_out)

    @pl.when(between)
    def _():
        pair_sent(N_PR, N_RS, n_pair)
        by_role(sent, N_AG, n_all)
        by_role(sent, Q_RS, q_out)

    @pl.when(jnp.logical_and(between, leads))
    def _():
        sent(C_SH, c_in.at[pl.ds(0, n - 1)])
        sent(D_SH, c_in.at[pl.ds(0, n - 1)])

        @pl.when(is_turn)
        def _():
            sent(C_ON, c_in)

        @pl.when(jnp.logical_and(s > 1, s < strips - 2))
        def _():
            sent(C_ON, c_out)

        @pl.when(is_direct)
        def _():
            sent(D_ON, c_in)

    @pl.when(is_last)
    def _():
        pair_sent(M_PR, M_RS, m_pair)
        sent(L_AG, m_all.at[pl.ds(0, leaders)])
        sent(R_RS, q_out)


def body(strips, n, rhs, inverse, dis_fwd, agg_fwd, phase_fwd, gain_fwd, dis_back, agg_back, phase_back, gain_back):
    _, angles, unk = rhs.shape
    modes = agg_fwd.shape[2]
    width = 256 if unk % 256 == 0 else unk
    blocks = unk // width
    leaders = n // 2
    rows, part = angles // leaders, modes // n
    hbm = pl.BlockSpec(memory_space=pl.ANY)
    vmem = pl.BlockSpec(memory_space=pltpu.VMEM)
    out = pltpu.VMEM((angles, unk), F32)
    base, cu, du = pl.pallas_call(
        functools.partial(kernel, strips, n, width),
        out_shape=(out,) * 3,
        in_specs=[hbm] * 10,
        out_specs=(vmem,) * 3,
        scratch_shapes=[
            pltpu.VMEM((angles, unk), BF),
            pltpu.VMEM((modes, unk), BF),
            pltpu.VMEM((modes, unk), BF),
            pltpu.VMEM((blocks, unk, width), BF),
            pltpu.VMEM((unk, modes), BF),
            pltpu.VMEM((unk, modes), BF),
            pltpu.VMEM((angles, unk), BF),
            pltpu.VMEM((modes, unk), BF),
            pltpu.VMEM((modes, unk), BF),
        ]
        + [pltpu.VMEM((2, leaders, part, modes), kind) for kind in (F32,) * 3 + (BF,) * 3]
        + [pltpu.VMEM((leaders, part, modes), BF)] * 6
        + [pltpu.VMEM((n, part, modes), BF)] * 4
        + [
            pltpu.VMEM((count, rows, modes), kind)
            for count, kind in ((leaders, F32), (leaders, BF), (n, BF)) * 2 + ((n, BF),) * 2
        ]
        + [pltpu.VMEM((rows, modes), BF), pltpu.VMEM((leaders, rows, modes), BF)] * 2
        + [pltpu.VMEM((4, 1, modes // 2), F32)] * 2
        + [pltpu.SemaphoreType.DMA((9 + blocks,)), pltpu.SemaphoreType.DMA((KINDS, 2))],
        compiler_params=pltpu.CompilerParams(
            collective_id=0, has_side_effects=True, vmem_limit_bytes=60 * 1024 * 1024
        ),
    )(rhs, inverse, dis_fwd, agg_fwd, phase_fwd, gain_fwd, dis_back, agg_back, phase_back, gain_back)
    first = base - cu
    return first[None], (first - du)[None]


def solution(mesh):
    strips, n = mesh.shape["strip"], mesh.shape["cross"]
    return jax.shard_map(
        functools.partial(body, strips, n),
        mesh=mesh,
        in_specs=(
            P("strip", None, "cross"),
            P("strip", "cross", None, None),
            P("strip", "cross", None, None),
            P("strip", "cross", None),
            P("strip", None),
            P("strip", None),
            P("strip", "cross", None, None),
            P("strip", "cross", None),
            P("strip", None),
            P("strip", None),
        ),
        out_specs=(P("strip", None, "cross"), P("strip", None, "cross")),
        check_vma=False,
    )
```
